256 devices in a mesh: slab: 4 (over x), range: 64 (over y, z, core).
Axes of the slice: x: 4, y: 4, z: 8, core: 2. Of those that a mesh axis runs over, the one named last changes fastest.
Arguments:
- features: bfloat16 [512, 512, 128], P(('slab', 'range')), may hold values from -54 to 54
- neighbours: int32 [512, 26], P(('slab', 'range')), may hold values from -1 to 9, as said below
- keep_mask: int32 [512, 8], P(('slab', 'range')), may hold values from 0 to 1, as said below
- owner: int32 [512, 8], P(('slab', 'range')), may hold values from 0 to 63, as said below
- norm_gain: float32 [4, 128], replicated, may hold values from 0.1 to 1.9
- norm_shift: float32 [4, 128], replicated, may hold values from -3 to 3
- conv_weights: bfloat16 [4, 27, 128, 128], replicated, may hold values from -0.109375 to 0.109375
- up_weight: bfloat16 [128, 512], replicated, may hold values from -0.5 to 0.5
Outputs:
- children: bfloat16 [32768, 64, 512], P(('slab', 'range'))
The draws below stay inside these ranges and needn't reach their ends.
Inputs may be any that keep to these rules, and one draw needn't show every extreme that they name: `neighbours`: entries are -1 (no neighbour) or q * 2 + slot as in the first step; directions whose first nonzero component is -1 use q in 0, 1, 3, the others q in 0, 2, 4; q = 3 only where dx = -1 and q = 4 only where dx = +1; no entry names a device outside the mesh. `keep_mask`: 1 keeps the child. Among the kept children of one device at most 2 have the same owner, and in every slab group one owner receives exactly 2 kept children from every device of the group.
All inputs are finite; a program needn't handle non-finite values.
Results may differ from the reference program's by a relative error of at most 0.013.
Values may be sent and summed in bfloat16 or wider, within the bound.
No kernel may reach another device: no remote copies, remote signals or barrier semaphores. Data moves between devices by JAX's collectives and lax.ppermute only.
A program may use at most 128 MiB of HBM per device.

```python
import math
import jax
import jax.numpy as jnp
from jax import lax

CHANNELS = 128
CHILD_CH = 64
GROUPS = 32
EDGE = 8
BLOCKS = 2
BRICK_DEV = 2
CAP = 2
SLAB_BRICKS = 128
BRICKS = 512
SLOTS = 32768
N_SLAB = 4
N_RANGE = 64


DIRECTIONS = [(first, second, third) for first in (-1, 0, 1) for second in (-1, 0, 1) for third in (-1, 0, 1) if (first, second, third) != (0, 0, 0)]


NEGATIVE = [[value for value in offsets if value != 0][0] < 0 for offsets in DIRECTIONS]


X_LOWER = [offsets[0] < 0 for offsets in DIRECTIONS]


X_UPPER = [offsets[0] > 0 for offsets in DIRECTIONS]


def draw_features(key, part):
    base_key, voxel_key, channel_key, common_key = jax.random.split(key, 4)
    shape = (BRICKS, EDGE ** 3, CHANNELS)
    voxel_scale = jnp.exp(jax.random.uniform(voxel_key, (BRICKS, EDGE ** 3, 1), jnp.float32, math.log(0.3), math.log(3.0)))
    channel_scale = jnp.exp(jax.random.uniform(channel_key, (1, 1, CHANNELS), jnp.float32, math.log(0.3), math.log(3.0)))
    base = jnp.clip(jax.random.normal(base_key, shape, jnp.float32), -6.0, 6.0)
    return (base * voxel_scale * channel_scale).astype(jnp.bfloat16)


def draw_neighbours(key, part):
    range_count = SLAB_BRICKS // BRICK_DEV
    slab_count = BRICKS // SLAB_BRICKS
    device = jnp.arange(BRICKS, dtype=jnp.int32) // BRICK_DEV
    slab_index = (device // range_count)[:, None]
    range_index = (device % range_count)[:, None]
    negative = jnp.array(NEGATIVE)[None, :]
    x_lower = jnp.array(X_LOWER)[None, :]
    x_upper = jnp.array(X_UPPER)[None, :]
    pick_key, slot_key = jax.random.split(key)
    pick = jax.random.randint(pick_key, (BRICKS, 26), 0, 100)
    slot_index = jax.random.randint(slot_key, (BRICKS, 26), 0, BRICK_DEV)
    range_open = jnp.where(negative, range_index > 0, range_index < range_count - 1)
    slab_open = x_lower & (slab_index > 0) | x_upper & (slab_index < slab_count - 1)
    range_source = jnp.where(negative, 1, 2)
    slab_source = jnp.where(negative, 3, 4)
    source = jnp.where(pick < 55, 0, jnp.where(pick < 80, jnp.where(range_open, range_source, 0), jnp.where(slab_open, slab_source, 0)))
    value = source * BRICK_DEV + slot_index
    return jnp.where(pick < 20, -1, value).astype(jnp.int32)


def route_plan(key):
    range_count = SLAB_BRICKS // BRICK_DEV
    devices = BRICKS // BRICK_DEV
    children = 8 * BRICK_DEV

    def one_device(device):
        slab_index = device // range_count
        home = jax.random.randint(jax.random.fold_in(key, 7000 + slab_index), (), 0, range_count)
        device_key = jax.random.fold_in(key, device)
        other_key, order_key, level_key, keep_key = jax.random.split(device_key, 4)
        others = jax.random.permutation(other_key, (range_count - 1) * CAP)
        other_peer = (home + 1 + others // CAP) % range_count
        slot_peer = jnp.concatenate([jnp.zeros((CAP,), jnp.int32) + home, other_peer.astype(jnp.int32)])[:children]
        order = jax.random.permutation(order_key, children)
        target = slot_peer[order]
        level = jax.random.randint(level_key, (), 60, 101)
        keep = (jax.random.randint(keep_key, (children,), 0, 100) < level) | (target == home)
        return (target.astype(jnp.int32), keep.astype(jnp.int32))
    targets, keeps = jax.vmap(one_device)(jnp.arange(devices, dtype=jnp.int32))
    return (targets.reshape(BRICKS, 8), keeps.reshape(BRICKS, 8))


def draw_owner(key, part):
    targets, keeps = route_plan(jax.random.fold_in(key, 11))
    return targets


def draw_keep_mask(key, part):
    targets, keeps = route_plan(jax.random.fold_in(key, 11))
    return keeps


def centred(rng, dims, width, limit, held_as=jnp.bfloat16):
    return jnp.clip(width * jax.random.normal(rng, dims, jnp.float32), -limit, limit).astype(held_as)


def setup_inputs(seed: int = 0) -> dict:
    streams_of = jax.random.split(jax.random.key(seed), 9)
    features = draw_features(jax.random.fold_in(streams_of[8], 71), 0)
    neighbours = draw_neighbours(jax.random.fold_in(streams_of[8], 71), 0)
    keep_mask = draw_keep_mask(jax.random.fold_in(streams_of[8], 71), 0)
    owner = draw_owner(jax.random.fold_in(streams_of[8], 71), 0)
    norm_gain = jnp.clip(1.0 + 0.18 * jax.random.normal(streams_of[4], (2 * BLOCKS, CHANNELS), jnp.float32), 0.1, 1.9)
    norm_shift = centred(streams_of[5], (2 * BLOCKS, CHANNELS), 0.5, 3.0, jnp.float32)
    conv_weights = centred(streams_of[6], (2 * BLOCKS, 27, CHANNELS, CHANNELS), (27 * CHANNELS) ** -0.5, 0.109375)
    up_weight = centred(streams_of[7], (CHANNELS, 8 * CHILD_CH), CHANNELS ** -0.5, 0.5)
    return dict(features=features, neighbours=neighbours, keep_mask=keep_mask, owner=owner, norm_gain=norm_gain, norm_shift=norm_shift, conv_weights=conv_weights, up_weight=up_weight)


DIRECTIONS = [(first, second, third) for first in (-1, 0, 1) for second in (-1, 0, 1) for third in (-1, 0, 1) if (first, second, third) != (0, 0, 0)]

def normalize(values, gain, shift):
    count, voxels, channels = values.shape
    wide = values.astype(jnp.float32).reshape(count, voxels, GROUPS, channels // GROUPS)
    center = lax.optimization_barrier(jnp.mean(wide, axis=(1, 3), keepdims=True))
    spread = lax.optimization_barrier(jnp.mean(jnp.square(wide - center), axis=(1, 3), keepdims=True))
    scaled = ((wide - center) * lax.rsqrt(spread + 1e-06)).reshape(count, voxels, channels)
    return jax.nn.silu(scaled * gain + shift).astype(jnp.bfloat16)

def neighbour_cut(offset, brick_edge):
    if offset < 0:
        return slice(brick_edge - 1, brick_edge)
    if offset > 0:
        return slice(0, 1)
    return slice(None)

def padded_place(offset, brick_edge):
    if offset < 0:
        return slice(0, 1)
    if offset > 0:
        return slice(brick_edge + 1, brick_edge + 2)
    return slice(1, brick_edge + 1)

def convolve(padded, weight):
    count = padded.shape[0]
    brick_edge = padded.shape[1] - 2
    channels = padded.shape[-1]
    total = jnp.zeros((count * brick_edge ** 3, weight.shape[-1]), jnp.float32)
    for shift_x in range(3):
        for shift_y in range(3):
            window = jnp.concatenate([padded[:, shift_x:shift_x + brick_edge, shift_y:shift_y + brick_edge, shift_z:shift_z + brick_edge] for shift_z in range(3)], axis=-1)
            first_tap = (shift_x * 3 + shift_y) * 3
            taps = weight[first_tap:first_tap + 3].reshape(3 * channels, weight.shape[-1])
            total = total + jnp.dot(window.reshape(-1, 3 * channels), taps, preferred_element_type=jnp.float32)
    return total

def normalize_all(state, gain, shift):
    count = BRICK_DEV * N_SLAB
    blocks = state.reshape(BRICKS // count, count, EDGE ** 3, CHANNELS)
    return lax.map(lambda part_state: normalize(part_state, gain, shift), blocks).reshape(BRICKS, EDGE ** 3, CHANNELS)

def convolve_all(active, neighbours, weight, residual):
    count = BRICK_DEV * N_SLAB
    volume = active.reshape(BRICKS, EDGE, EDGE, EDGE, CHANNELS)
    pieces = [volume[:, neighbour_cut(offsets[0], EDGE), neighbour_cut(offsets[1], EDGE), neighbour_cut(offsets[2], EDGE)] for offsets in DIRECTIONS]

    def one_block(index):
        start = index * count
        own = lax.dynamic_slice_in_dim(volume, start, count, 0)
        entries = lax.dynamic_slice_in_dim(neighbours, start, count, 0)
        device = (start + jnp.arange(count, dtype=jnp.int32)) // BRICK_DEV
        padded = jnp.pad(own, ((0, 0), (1, 1), (1, 1), (1, 1), (0, 0)))
        for position, offsets in enumerate(DIRECTIONS):
            entry = entries[:, position]
            source = entry // BRICK_DEV
            sender = jnp.where(source == 1, device - 1, jnp.where(source == 2, device + 1, jnp.where(source == 3, device - N_RANGE, jnp.where(source == 4, device + N_RANGE, device))))
            target = jnp.clip(sender * BRICK_DEV + entry % BRICK_DEV, 0, BRICKS - 1).astype(jnp.int32)
            picked = jnp.take(pieces[position], target, axis=0)
            picked = jnp.where((entry >= 0)[:, None, None, None, None], picked, jnp.zeros_like(picked))
            padded = padded.at[:, padded_place(offsets[0], EDGE), padded_place(offsets[1], EDGE), padded_place(offsets[2], EDGE)].set(picked)
        total = convolve(padded, weight)
        if residual is not None:
            total = lax.dynamic_slice_in_dim(residual, start, count, 0).astype(jnp.float32).reshape(-1, CHANNELS) + total
        return total.astype(jnp.bfloat16)
    return lax.map(one_block, jnp.arange(BRICKS // count, dtype=jnp.int32)).reshape(BRICKS, EDGE ** 3, CHANNELS)

def reference(features, neighbours, keep_mask, owner, norm_gain, norm_shift, conv_weights, up_weight):
    state = features
    for block in range(BLOCKS):
        active = normalize_all(state, norm_gain[2 * block], norm_shift[2 * block])
        hidden = convolve_all(active, neighbours, conv_weights[2 * block], None)
        active = normalize_all(hidden, norm_gain[2 * block + 1], norm_shift[2 * block + 1])
        state = convolve_all(active, neighbours, conv_weights[2 * block + 1], state)
    devices = BRICKS // BRICK_DEV
    children = 8 * BRICK_DEV
    half_edge = EDGE // 2
    octants = state.reshape(BRICKS, 2, half_edge, 2, half_edge, 2, half_edge, CHANNELS)
    octants = octants.transpose(0, 1, 3, 5, 2, 4, 6, 7).reshape(BRICKS * 8, half_edge ** 3, CHANNELS)
    kept = keep_mask.reshape(devices, children)
    target = owner.reshape(devices, children)
    hits = ((target[:, :, None] == jnp.arange(N_RANGE, dtype=jnp.int32)[None, None, :]) & (kept[:, :, None] == 1)).astype(jnp.int32)
    rank = lax.optimization_barrier(jnp.sum((jnp.cumsum(hits, axis=1) - hits) * hits, axis=2)).astype(jnp.int32)
    device = jnp.arange(devices, dtype=jnp.int32)[:, None]
    slot_row = ((device // N_RANGE * N_RANGE + target) * N_RANGE + device % N_RANGE) * CAP + rank
    slot_row = jnp.where(kept == 1, slot_row, SLOTS).reshape(-1).astype(jnp.int32)
    placed = jnp.zeros((SLOTS, half_edge ** 3, CHANNELS), jnp.bfloat16).at[slot_row].set(octants, mode='drop')

    def grow(block):
        return jnp.dot(block.reshape(-1, CHANNELS), up_weight, preferred_element_type=jnp.float32).astype(jnp.bfloat16)
    grown = lax.map(grow, placed.reshape(devices, SLOTS // devices, half_edge ** 3, CHANNELS))
    return grown.reshape(SLOTS, half_edge ** 3, 8 * CHILD_CH)
```

```python
import functools

import jax
import jax.numpy as jnp
from jax import lax
from jax.experimental import pallas as pl
from jax.experimental.pallas import tpu as pltpu
from jax.sharding import PartitionSpec as P

EDGE = 8
CH = 128
BRICKS = 2
VOX = EDGE**3
OCT = 64
PITCH = 24
FACE = EDGE * EDGE
DIRECTIONS = [
    (dx, dy, dz)
    for dx in (-1, 0, 1)
    for dy in (-1, 0, 1)
    for dz in (-1, 0, 1)
    if (dx, dy, dz) != (0, 0, 0)
]
OWN_HI, OWN_LO, CORE, RANGE, SLAB_A, SLAB_B, ZERO = 0, 6, 12, 18, 24, 26, 28
FACES = 29

VMEM = pl.BlockSpec(memory_space=pltpu.VMEM)
SMEM = pl.BlockSpec(memory_space=pltpu.SMEM)
ANY = pl.BlockSpec(memory_space=pl.ANY)


def group_sum(rows):
    lane = lax.broadcasted_iota(jnp.int32, rows.shape, 1)
    pair = jnp.where(lane % 2 == 0, pltpu.roll(rows, CH - 1, 1), pltpu.roll(rows, 1, 1))
    rows = rows + pair
    pair = jnp.where(lane % 4 < 2, pltpu.roll(rows, CH - 2, 1), pltpu.roll(rows, 2, 1))
    return jnp.sum(rows + pair, axis=0, keepdims=True)


def normalize(load, gain, shift):
    size = VOX * 4.0
    mean = group_sum(jnp.sum(load(), axis=0)) / size
    centred = load() - mean
    spread = group_sum(jnp.sum(centred * centred, axis=0)) / size
    scale = lax.rsqrt(spread + 1e-6) * gain
    w = (load() - mean) * scale + shift
    return w * (0.5 + 0.5 * jnp.tanh(0.5 * w))


def emit_active(load, b, gain, shift, info, act_s, act, sends):
    value = normalize(load, gain, shift)
    act_s[pl.ds(b * VOX, VOX)] = value.reshape(VOX, CH)
    act[b] = value.reshape(VOX, CH).astype(jnp.bfloat16)
    last, first, to_core, to_range, to_a, to_b = sends
    base = b * VOX
    for x in range(EDGE):
        rows = pl.ds(x * EDGE, EDGE)
        for side, plane in ((7, last), (0, first)):
            plane[0, b, rows] = act_s[pl.ds(base + side * 64 + x * 8, 8)].astype(jnp.bfloat16)
            plane[1, b, rows] = act_s[pl.ds(base + x * 64 + side * 8, 8)].astype(jnp.bfloat16)
            plane[2, b, rows] = act_s[pl.ds(base + x * 64 + side, 8, stride=8)].astype(jnp.bfloat16)


def choose_sends(info, sends):
    last, first, to_core, to_range, to_a, to_b = sends

    def route(flag, yes, no):
        @pl.when(flag == 0)
        def _():
            yes[...] = last[...] if yes.shape[0] == 3 else last[0]
            no[...] = first[...] if no.shape[0] == 3 else first[0]

        @pl.when(flag != 0)
        def _():
            yes[...] = first[...] if yes.shape[0] == 3 else first[0]
            no[...] = last[...] if no.shape[0] == 3 else last[0]

    route(info[0], to_core, to_range)
    route(info[1], to_a, to_b)


def start_kernel(
    info, features, neighbours, kept, owner, gain, shift,
    act, last, first, to_core, to_range, to_a, to_b, faces, slots, act_s,
):
    sends = (last, first, to_core, to_range, to_a, to_b)
    for b in range(BRICKS):
        load = lambda b=b: features[b].astype(jnp.float32).reshape(OCT, EDGE, CH)
        emit_active(load, b, gain[0:1], shift[0:1], info, act_s, act, sends)
    choose_sends(info, sends)
    odd_range, odd_slab = info[0], info[1]
    below = jnp.where(odd_range == 1, CORE, RANGE)
    above = jnp.where(odd_range == 1, RANGE, CORE)
    under = jnp.where(odd_slab == 1, SLAB_A, SLAB_B)
    over = jnp.where(odd_slab == 1, SLAB_B, SLAB_A)
    for b in range(BRICKS):
        for k, offsets in enumerate(DIRECTIONS):
            axis = [a for a in range(3) if offsets[a] != 0][0]
            negative = offsets[axis] < 0
            entry = neighbours[b, k]
            source = entry // BRICKS
            own, side, slab = (OWN_HI, below, under) if negative else (OWN_LO, above, over)
            near = jnp.where(source == 0, own, side) + axis * BRICKS
            face = jnp.where(source > 2, slab, near) + entry % BRICKS
            face = jnp.where(entry < 0, ZERO, jnp.clip(face, 0, ZERO))
            faces[b, k] = face * FACE
    owners = [owner[c // 8, c % 8] for c in range(8 * BRICKS)]
    keeps = [kept[c // 8, c % 8] for c in range(8 * BRICKS)]
    for c in range(8 * BRICKS):
        rank = jnp.int32(0)
        for e in range(c):
            same = (owners[e] == owners[c]) & (keeps[e] == 1)
            rank = rank + jnp.where(same, 1, 0)
        slot = jnp.clip(owners[c] * 2 + jnp.minimum(rank, 1), 0, 127)
        slots[c] = jnp.where(keeps[c] == 1, slot, -1)


def assemble(act, faces, planes, table, field, window):
    row = 0
    for plane in planes:
        whole = plane[...].astype(jnp.float32)
        count = whole.size // CH
        table[pl.ds(row, count)] = whole.reshape(count, CH)
        row += count
    table[pl.ds(ZERO * FACE, FACE)] = jnp.zeros((FACE, CH), jnp.float32)

    def cell(x, y, b):
        return ((x * 10 + y) * BRICKS + b) * PITCH

    for b in range(BRICKS):
        for x in range(EDGE):
            for y in range(EDGE):
                tile = act[b, pl.ds((x * 8 + y) * 8, 8)].astype(jnp.float32)
                field[pl.ds(cell(x + 1, y + 1, b) + 8, 8)] = tile
    for b in range(BRICKS):
        for k, (dx, dy, dz) in enumerate(DIRECTIONS):
            base = pl.multiple_of(faces[b, k], FACE)
            cut = lambda d: 7 if d < 0 else 0
            put = lambda d: 0 if d < 0 else 9
            deep = 7 if dz < 0 else 16
            if dx != 0:
                px = put(dx)
                ys = range(EDGE) if dy == 0 else [None]
                if dz == 0:
                    for y in ys:
                        sy, py = (y, y + 1) if dy == 0 else (cut(dy), put(dy))
                        field[pl.ds(cell(px, py, b) + 8, 8)] = table[pl.ds(base + sy * 8, 8)]
                elif dy == 0:
                    column = table[pl.ds(base + cut(dz), 8, stride=8)]
                    field[pl.ds(cell(px, 1, b) + deep, 8, stride=BRICKS * PITCH)] = column
                else:
                    corner = table[pl.ds(base + cut(dy) * 8 + cut(dz), 1)]
                    field[pl.ds(cell(px, put(dy), b) + deep, 1)] = corner
            elif dy != 0:
                py = put(dy)
                if dz == 0:
                    for x in range(EDGE):
                        field[pl.ds(cell(x + 1, py, b) + 8, 8)] = table[pl.ds(base + x * 8, 8)]
                else:
                    column = table[pl.ds(base + cut(dz), 8, stride=8)]
                    field[pl.ds(cell(1, py, b) + deep, 8, stride=10 * BRICKS * PITCH)] = column
            else:
                for x in range(EDGE):
                    rows = table[pl.ds(base + x * 8, 8)]
                    field[pl.ds(cell(x + 1, 1, b) + deep, 8, stride=BRICKS * PITCH)] = rows
    for x in range(10):
        for y in range(10):
            for w in range(3):
                tile = jnp.concatenate(
                    [field[pl.ds(cell(x, y, b) + 7 + w, 8)] for b in range(BRICKS)], axis=0
                )
                window[x, y, :, w * CH : (w + 1) * CH] = tile.astype(jnp.bfloat16)


def convolve(window, weights, total):
    for p in range(3):
        rows = jnp.concatenate([window[p : p + 8, t : t + 8] for t in range(3)], axis=-1)
        part = jnp.dot(
            rows.reshape(BRICKS * VOX, 9 * CH),
            weights[p * 9 * CH : (p + 1) * 9 * CH],
            preferred_element_type=jnp.float32,
        ).reshape(OCT, BRICKS, EDGE, CH)
        if p == 0:
            total[...] = part
        else:
            total[...] += part


def conv_kernel(
    step, info, faces, act, last, first, core, rng, slab_a, slab_b, weights_hbm, gain, shift, *rest,
):
    rest = list(rest)
    state = rest.pop(0) if step % 2 else None
    slots = rest.pop(0) if step == 3 else None
    if step == 3:
        packed = rest.pop(0)
    else:
        act_out = rest.pop(0)
        sends = [rest.pop(0) for _ in range(6)]
        state_out = rest.pop(0) if step == 1 else None
    table, field, window, weights, total, act_s, sem = rest
    copy = pltpu.make_async_copy(weights_hbm.at[step], weights, sem)
    copy.start()
    assemble(act, faces, (last, first, core, rng, slab_a, slab_b), table, field, window)
    if step == 3:
        packed[...] = jnp.zeros(packed.shape, packed.dtype)
    copy.wait()
    convolve(window, weights, total)
    for b in range(BRICKS):
        if step % 2:
            value = total[:, b] + state[b].astype(jnp.float32).reshape(OCT, EDGE, CH)
            value = value.astype(jnp.bfloat16)
            if step == 1:
                state_out[b] = value.reshape(VOX, CH)
            total[:, b] = value.astype(jnp.float32)
        else:
            total[:, b] = total[:, b].astype(jnp.bfloat16).astype(jnp.float32)
        if step < 3:
            load = lambda b=b: total[:, b]
            emit_active(load, b, gain[step + 1 : step + 2], shift[step + 1 : step + 2], info, act_s, act_out, sends)
    if step < 3:
        choose_sends(info, sends)
        return
    low = lax.broadcasted_iota(jnp.int32, (4, 2, 8, CH), 2) < 4
    for b in range(BRICKS):
        for ox in range(2):
            for oy in range(2):
                tiles = total[pl.ds(ox * 32, 32), b].reshape(4, 8, EDGE, CH)
                tiles = tiles[:, oy * 4 : oy * 4 + 4].reshape(4, 2, 2, EDGE, CH)
                even, odd = tiles[:, :, 0], tiles[:, :, 1]
                turn = lambda v: pltpu.roll(v.reshape(8, EDGE, CH), 4, 1).reshape(4, 2, EDGE, CH)
                for oz in range(2):
                    block = jnp.where(low, even, turn(odd)) if oz == 0 else jnp.where(low, turn(even), odd)
                    child = b * 8 + (ox * 2 + oy) * 2 + oz
                    block = block.reshape(OCT, CH).astype(jnp.bfloat16)
                    slot = slots[child]

                    @pl.when(slot >= 0)
                    def _(slot=slot, block=block):
                        packed[slot] = block


def grow_kernel(octants, up, out):
    rows = octants[...].reshape(-1, CH)
    grown = jnp.dot(rows, up[...], preferred_element_type=jnp.float32)
    out[...] = grown.astype(jnp.bfloat16).reshape(out.shape)


def bf16(*shape):
    return jax.ShapeDtypeStruct(shape, jnp.bfloat16)


def swap(block, axis, odd):
    count = lax.axis_size(axis)
    route = []
    for i in range(count):
        j = (i ^ 1) if not odd else (i + 1 if i % 2 else i - 1)
        if 0 <= j < count:
            route.append((i, j))
    return lax.ppermute(block, axis, route)


def exchange(sends):
    last, first, to_core, to_range, to_a, to_b = sends
    return (
        last,
        first,
        swap(to_core, "range", False),
        swap(to_range, "range", True),
        swap(to_a, "slab", False),
        swap(to_b, "slab", True),
    )


SENDS = [
    bf16(3, BRICKS, FACE, CH),
    bf16(3, BRICKS, FACE, CH),
    bf16(3, BRICKS, FACE, CH),
    bf16(3, BRICKS, FACE, CH),
    bf16(BRICKS, FACE, CH),
    bf16(BRICKS, FACE, CH),
]
LIMIT = 48 * 1024 * 1024


def shards(features, neighbours, keep_mask, owner, norm_gain, norm_shift, conv_weights, up_weight):
    info = jnp.stack([lax.axis_index("range") % 2, lax.axis_index("slab") % 2]).astype(jnp.int32)
    act_s = pltpu.VMEM((BRICKS * VOX, CH), jnp.float32)
    act, *sends, faces, slots = pl.pallas_call(
        start_kernel,
        out_shape=[bf16(BRICKS, VOX, CH), *SENDS, jax.ShapeDtypeStruct((BRICKS, 26), jnp.int32),
                   jax.ShapeDtypeStruct((8 * BRICKS,), jnp.int32)],
        in_specs=[SMEM, VMEM, SMEM, SMEM, SMEM, VMEM, VMEM],
        out_specs=[VMEM] * 7 + [SMEM, SMEM],
        scratch_shapes=[act_s],
        name="start",
    )(info, features, neighbours, keep_mask, owner, norm_gain, norm_shift)
    weights = conv_weights.reshape(4, 27 * CH, CH)
    state = features
    for step in range(4):
        planes = exchange(sends)
        inputs = [info, faces, act, *planes, weights, norm_gain, norm_shift]
        in_specs = [SMEM, SMEM] + [VMEM] * 7 + [ANY, VMEM, VMEM]
        if step % 2:
            inputs.append(state)
            in_specs.append(VMEM)
        if step == 3:
            inputs.append(slots)
            in_specs.append(SMEM)
            outs = [bf16(128, OCT, CH)]
        else:
            outs = [bf16(BRICKS, VOX, CH), *SENDS]
            if step == 1:
                outs.append(bf16(BRICKS, VOX, CH))
        result = pl.pallas_call(
            functools.partial(conv_kernel, step),
            out_shape=outs,
            in_specs=in_specs,
            out_specs=[VMEM] * len(outs),
            scratch_shapes=[
                pltpu.VMEM((FACES * FACE, CH), jnp.float32),
                pltpu.VMEM((100 * BRICKS * PITCH, CH), jnp.float32),
                pltpu.VMEM((10, 10, BRICKS * EDGE, 3 * CH), jnp.bfloat16),
                pltpu.VMEM((27 * CH, CH), jnp.bfloat16),
                pltpu.VMEM((OCT, BRICKS, EDGE, CH), jnp.float32),
                act_s,
                pltpu.SemaphoreType.DMA,
            ],
            compiler_params=pltpu.CompilerParams(vmem_limit_bytes=LIMIT),
            name=f"conv{step}",
        )(*inputs)
        if step < 3:
            act, sends = result[0], result[1:7]
            if step == 1:
                state = result[7]
    arrived = lax.all_to_all(result[0], "range", split_axis=0, concat_axis=0, tiled=True)
    slab = 8
    return pl.pallas_call(
        grow_kernel,
        grid=(128 // slab,),
        out_shape=bf16(128, OCT, 4 * CH),
        in_specs=[
            pl.BlockSpec((slab, OCT, CH), lambda i: (i, 0, 0)),
            pl.BlockSpec((CH, 4 * CH), lambda i: (0, 0)),
        ],
        out_specs=pl.BlockSpec((slab, OCT, 4 * CH), lambda i: (i, 0, 0)),
        name="grow",
    )(arrived, up_weight)


def solution(mesh):
    split = P(("slab", "range"))
    return jax.shard_map(
        shards,
        mesh=mesh,
        in_specs=(split, split, split, split, P(), P(), P(), P()),
        out_specs=split,
        check_vma=False,
    )
```

```python
import functools

import jax
import jax.numpy as jnp
from jax import lax
from jax.experimental import pallas as pl
from jax.experimental.pallas import tpu as pltpu
from jax.sharding import PartitionSpec as P

EDGE = 8
CH = 128
BRICKS = 2
VOX = EDGE**3
OCT = 64
PITCH = 24
FACE = EDGE * EDGE
DIRECTIONS = [
    (dx, dy, dz)
    for dx in (-1, 0, 1)
    for dy in (-1, 0, 1)
    for dz in (-1, 0, 1)
    if (dx, dy, dz) != (0, 0, 0)
]
OWN_HI, OWN_LO, CORE, RANGE, SLAB_A, SLAB_B, ZERO = 0, 6, 12, 18, 24, 26, 28
FACES = 29

VMEM = pl.BlockSpec(memory_space=pltpu.VMEM)
SMEM = pl.BlockSpec(memory_space=pltpu.SMEM)
ANY = pl.BlockSpec(memory_space=pl.ANY)
HBM = pl.BlockSpec(memory_space=pltpu.HBM)


def group_sum(rows):
    lane = lax.broadcasted_iota(jnp.int32, rows.shape, 1)
    pair = jnp.where(lane % 2 == 0, pltpu.roll(rows, CH - 1, 1), pltpu.roll(rows, 1, 1))
    rows = rows + pair
    pair = jnp.where(lane % 4 < 2, pltpu.roll(rows, CH - 2, 1), pltpu.roll(rows, 2, 1))
    return jnp.sum(rows + pair, axis=0, keepdims=True)


def normalize(load, gain, shift):
    size = VOX * 4.0
    mean = group_sum(jnp.sum(load(), axis=0)) / size
    centred = load() - mean
    spread = group_sum(jnp.sum(centred * centred, axis=0)) / size
    scale = lax.rsqrt(spread + 1e-6) * gain
    w = (load() - mean) * scale + shift
    return w * (0.5 + 0.5 * jnp.tanh(0.5 * w))


def emit_active(load, b, gain, shift, act_s, act, sends):
    value = normalize(load, gain, shift)
    act_s[pl.ds(b * VOX, VOX)] = value.reshape(VOX, CH)
    act[b] = value.reshape(VOX, CH).astype(jnp.bfloat16)
    last, first, to_core, to_range, to_a, to_b = sends
    base = b * VOX
    for x in range(EDGE):
        rows = pl.ds(x * EDGE, EDGE)
        for side, plane in ((7, last), (0, first)):
            plane[0, b, rows] = act_s[pl.ds(base + side * 64 + x * 8, 8)].astype(jnp.bfloat16)
            plane[1, b, rows] = act_s[pl.ds(base + x * 64 + side * 8, 8)].astype(jnp.bfloat16)
            plane[2, b, rows] = act_s[pl.ds(base + x * 64 + side, 8, stride=8)].astype(jnp.bfloat16)


def parity(axis):
    return lax.rem(lax.axis_index(axis), 2)


def choose_sends(sends):
    last, first, to_core, to_range, to_a, to_b = sends

    def route(flag, yes, no):
        @pl.when(flag == 0)
        def _():
            yes[...] = last[...] if yes.shape[0] == 3 else last[0]
            no[...] = first[...] if no.shape[0] == 3 else first[0]

        @pl.when(flag != 0)
        def _():
            yes[...] = first[...] if yes.shape[0] == 3 else first[0]
            no[...] = last[...] if no.shape[0] == 3 else last[0]

    route(parity("range"), to_core, to_range)
    route(parity("slab"), to_a, to_b)


def fetch(sems, *pairs):
    copies = [pltpu.make_async_copy(src, dst, sems.at[i]) for i, (src, dst) in enumerate(pairs)]
    for copy in copies:
        copy.start()
    return copies


def start_kernel(
    features_hbm, gain_hbm, shift_hbm, act, last, first, to_core, to_range, to_a, to_b,
    act_s, features, gain, shift, sems,
):
    copies = fetch(sems, (gain_hbm, gain), (shift_hbm, shift), *[(features_hbm.at[b], features.at[b]) for b in range(BRICKS)])
    for copy in copies[:2]:
        copy.wait()
    sends = (last, first, to_core, to_range, to_a, to_b)
    for b in range(BRICKS):
        copies[2 + b].wait()
        load = lambda b=b: features[b].astype(jnp.float32).reshape(OCT, EDGE, CH)
        emit_active(load, b, gain[0:1], shift[0:1], act_s, act, sends)
    choose_sends(sends)


def route_kernel(neighbours_hbm, kept_hbm, owner_hbm, after, faces, slots, neighbours, kept, owner, sems):
    for copy in fetch(sems, (neighbours_hbm, neighbours), (kept_hbm, kept), (owner_hbm, owner)):
        copy.wait()
    odd_range, odd_slab = parity("range"), parity("slab")
    below = jnp.where(odd_range == 1, CORE, RANGE)
    above = jnp.where(odd_range == 1, RANGE, CORE)
    under = jnp.where(odd_slab == 1, SLAB_A, SLAB_B)
    over = jnp.where(odd_slab == 1, SLAB_B, SLAB_A)
    for b in range(BRICKS):
        for k, offsets in enumerate(DIRECTIONS):
            axis = [a for a in range(3) if offsets[a] != 0][0]
            negative = offsets[axis] < 0
            entry = neighbours[b, k]
            source = entry // BRICKS
            own, side, slab = (OWN_HI, below, under) if negative else (OWN_LO, above, over)
            near = jnp.where(source == 0, own, side) + axis * BRICKS
            face = jnp.where(source > 2, slab, near) + entry % BRICKS
            face = jnp.where(entry < 0, ZERO, jnp.clip(face, 0, ZERO))
            faces[b, k] = face * FACE
    owners = [owner[c // 8, c % 8] for c in range(8 * BRICKS)]
    keeps = [kept[c // 8, c % 8] for c in range(8 * BRICKS)]
    for c in range(8 * BRICKS):
        rank = jnp.int32(0)
        for e in range(c):
            same = (owners[e] == owners[c]) & (keeps[e] == 1)
            rank = rank + jnp.where(same, 1, 0)
        slot = jnp.clip(owners[c] * 2 + jnp.minimum(rank, 1), 0, 127)
        slots[c] = jnp.where(keeps[c] == 1, slot, -1)


def assemble(act, faces, planes, table, field, window):
    row = 0
    for plane in planes:
        whole = plane[...].astype(jnp.float32)
        count = whole.size // CH
        table[pl.ds(row, count)] = whole.reshape(count, CH)
        row += count
    table[pl.ds(ZERO * FACE, FACE)] = jnp.zeros((FACE, CH), jnp.float32)

    def cell(x, y, b):
        return ((x * 10 + y) * BRICKS + b) * PITCH

    for b in range(BRICKS):
        for x in range(EDGE):
            for y in range(EDGE):
                tile = act[b, pl.ds((x * 8 + y) * 8, 8)].astype(jnp.float32)
                field[pl.ds(cell(x + 1, y + 1, b) + 8, 8)] = tile
    for b in range(BRICKS):
        for k, (dx, dy, dz) in enumerate(DIRECTIONS):
            base = pl.multiple_of(faces[b, k], FACE)
            cut = lambda d: 7 if d < 0 else 0
            put = lambda d: 0 if d < 0 else 9
            deep = 7 if dz < 0 else 16
            if dx != 0:
                px = put(dx)
                ys = range(EDGE) if dy == 0 else [None]
                if dz == 0:
                    for y in ys:
                        sy, py = (y, y + 1) if dy == 0 else (cut(dy), put(dy))
                        field[pl.ds(cell(px, py, b) + 8, 8)] = table[pl.ds(base + sy * 8, 8)]
                elif dy == 0:
                    column = table[pl.ds(base + cut(dz), 8, stride=8)]
                    field[pl.ds(cell(px, 1, b) + deep, 8, stride=BRICKS * PITCH)] = column
                else:
                    corner = table[pl.ds(base + cut(dy) * 8 + cut(dz), 1)]
                    field[pl.ds(cell(px, put(dy), b) + deep, 1)] = corner
            elif dy != 0:
                py = put(dy)
                if dz == 0:
                    for x in range(EDGE):
                        field[pl.ds(cell(x + 1, py, b) + 8, 8)] = table[pl.ds(base + x * 8, 8)]
                else:
                    column = table[pl.ds(base + cut(dz), 8, stride=8)]
                    field[pl.ds(cell(1, py, b) + deep, 8, stride=10 * BRICKS * PITCH)] = column
            else:
                for x in range(EDGE):
                    rows = table[pl.ds(base + x * 8, 8)]
                    field[pl.ds(cell(x + 1, 1, b) + deep, 8, stride=BRICKS * PITCH)] = rows
    for x in range(10):
        for y in range(10):
            for w in range(3):
                tile = jnp.concatenate(
                    [field[pl.ds(cell(x, y, b) + 7 + w, 8)] for b in range(BRICKS)], axis=0
                )
                window[x, y, :, w * CH : (w + 1) * CH] = tile.astype(jnp.bfloat16)


def convolve(window, weights, total):
    for p in range(3):
        rows = jnp.concatenate([window[p : p + 8, t : t + 8] for t in range(3)], axis=-1)
        part = jnp.dot(
            rows.reshape(BRICKS * VOX, 9 * CH),
            weights[p * 9 * CH : (p + 1) * 9 * CH],
            preferred_element_type=jnp.float32,
        ).reshape(OCT, BRICKS, EDGE, CH)
        if p == 0:
            total[...] = part
        else:
            total[...] += part


def conv_kernel(
    step, faces, act, last, first, core, rng, slab_a, slab_b, weights_hbm, gain_hbm, shift_hbm, *rest,
):
    rest = list(rest)
    state = rest.pop(0) if step % 2 else None
    slots = rest.pop(0) if step == 3 else None
    if step == 3:
        packed = rest.pop(0)
    else:
        act_out = rest.pop(0)
        sends = [rest.pop(0) for _ in range(6)]
        state_out = rest.pop(0) if step == 1 else None
    table, field, window, weights, total, act_s, gain, shift, sems = rest
    pairs = [(weights_hbm.at[step], weights)]
    if step < 3:
        pairs += [(gain_hbm, gain), (shift_hbm, shift)]
    copies = fetch(sems, *pairs)
    assemble(act, faces, (last, first, core, rng, slab_a, slab_b), table, field, window)
    if step == 3:
        packed[...] = jnp.zeros(packed.shape, packed.dtype)
    for copy in copies:
        copy.wait()
    convolve(window, weights, total)
    for b in range(BRICKS):
        if step % 2:
            value = total[:, b] + state[b].astype(jnp.float32).reshape(OCT, EDGE, CH)
            value = value.astype(jnp.bfloat16)
            if step == 1:
                state_out[b] = value.reshape(VOX, CH)
            total[:, b] = value.astype(jnp.float32)
        else:
            total[:, b] = total[:, b].astype(jnp.bfloat16).astype(jnp.float32)
        if step < 3:
            load = lambda b=b: total[:, b]
            emit_active(load, b, gain[step + 1 : step + 2], shift[step + 1 : step + 2], act_s, act_out, sends)
    if step < 3:
        choose_sends(sends)
        return
    low = lax.broadcasted_iota(jnp.int32, (4, 2, 8, CH), 2) < 4
    for b in range(BRICKS):
        for ox in range(2):
            for oy in range(2):
                tiles = total[pl.ds(ox * 32, 32), b].reshape(4, 8, EDGE, CH)
                tiles = tiles[:, oy * 4 : oy * 4 + 4].reshape(4, 2, 2, EDGE, CH)
                even, odd = tiles[:, :, 0], tiles[:, :, 1]
                turn = lambda v: pltpu.roll(v.reshape(8, EDGE, CH), 4, 1).reshape(4, 2, EDGE, CH)
                for oz in range(2):
                    block = jnp.where(low, even, turn(odd)) if oz == 0 else jnp.where(low, turn(even), odd)
                    child = b * 8 + (ox * 2 + oy) * 2 + oz
                    block = block.reshape(OCT, CH).astype(jnp.bfloat16)
                    slot = slots[child]

                    @pl.when(slot >= 0)
                    def _(slot=slot, block=block):
                        packed[slot] = block


def grow_kernel(octants, up, out):
    rows = octants[...].reshape(-1, CH)
    grown = jnp.dot(rows, up[...], preferred_element_type=jnp.float32)
    out[...] = grown.astype(jnp.bfloat16).reshape(out.shape)


def bf16(*shape):
    return jax.ShapeDtypeStruct(shape, jnp.bfloat16)


def swap(block, axis, odd):
    count = lax.axis_size(axis)
    route = []
    for i in range(count):
        j = (i ^ 1) if not odd else (i + 1 if i % 2 else i - 1)
        route.append((i, j % count))
    return lax.ppermute(block, axis, route)


def exchange(sends):
    last, first, to_core, to_range, to_a, to_b = sends
    return (
        last,
        first,
        swap(to_core, "range", False),
        swap(to_range, "range", True),
        swap(to_a, "slab", False),
        swap(to_b, "slab", True),
    )


SENDS = [
    bf16(3, BRICKS, FACE, CH),
    bf16(3, BRICKS, FACE, CH),
    bf16(3, BRICKS, FACE, CH),
    bf16(3, BRICKS, FACE, CH),
    bf16(BRICKS, FACE, CH),
    bf16(BRICKS, FACE, CH),
]
LIMIT = 16 * 1024 * 1024


def shards(features, neighbours, keep_mask, owner, norm_gain, norm_shift, conv_weights, up_weight):
    act_s = pltpu.VMEM((BRICKS * VOX, CH), jnp.float32)
    norm_s = [pltpu.VMEM((4, CH), jnp.float32)] * 2
    in_hbm = lambda v: pltpu.with_memory_space_constraint(v, pltpu.HBM)
    gain, shift = in_hbm(norm_gain), in_hbm(norm_shift)
    act, *sends = pl.pallas_call(
        start_kernel,
        out_shape=[bf16(BRICKS, VOX, CH), *SENDS],
        in_specs=[HBM] * 3,
        out_specs=[VMEM] * 7,
        scratch_shapes=[
            act_s,
            pltpu.VMEM((BRICKS, VOX, CH), jnp.bfloat16),
            *norm_s,
            pltpu.SemaphoreType.DMA((2 + BRICKS,)),
        ],
        compiler_params=pltpu.CompilerParams(vmem_limit_bytes=LIMIT),
        cost_estimate=pl.CostEstimate(flops=10**7, bytes_accessed=2**22, transcendentals=2**17),
        name="start",
    )(in_hbm(features), gain, shift)
    faces, slots = pl.pallas_call(
        route_kernel,
        out_shape=[jax.ShapeDtypeStruct((BRICKS, 26), jnp.int32), jax.ShapeDtypeStruct((8 * BRICKS,), jnp.int32)],
        in_specs=[HBM, HBM, HBM, ANY],
        out_specs=[SMEM, SMEM],
        scratch_shapes=[
            pltpu.SMEM((BRICKS, 26), jnp.int32),
            pltpu.SMEM((BRICKS, 8), jnp.int32),
            pltpu.SMEM((BRICKS, 8), jnp.int32),
            pltpu.SemaphoreType.DMA((3,)),
        ],
        compiler_params=pltpu.CompilerParams(vmem_limit_bytes=LIMIT),
        cost_estimate=pl.CostEstimate(flops=1000, bytes_accessed=4096, transcendentals=0),
        name="route",
    )(in_hbm(neighbours), in_hbm(keep_mask), in_hbm(owner), act)
    weights = in_hbm(conv_weights.reshape(4, 27 * CH, CH))
    state = features
    for step in range(4):
        planes = exchange(sends)
        inputs = [faces, act, *planes, weights, gain, shift]
        in_specs = [SMEM] + [VMEM] * 7 + [HBM] * 3
        if step % 2:
            inputs.append(state)
            in_specs.append(VMEM)
        if step == 3:
            inputs.append(slots)
            in_specs.append(SMEM)
            outs = [bf16(128, OCT, CH)]
        else:
            outs = [bf16(BRICKS, VOX, CH), *SENDS]
            if step == 1:
                outs.append(bf16(BRICKS, VOX, CH))
        result = pl.pallas_call(
            functools.partial(conv_kernel, step),
            out_shape=outs,
            in_specs=in_specs,
            out_specs=[VMEM] * len(outs),
            scratch_shapes=[
                pltpu.VMEM((FACES * FACE, CH), jnp.float32),
                pltpu.VMEM((100 * BRICKS * PITCH, CH), jnp.float32),
                pltpu.VMEM((10, 10, BRICKS * EDGE, 3 * CH), jnp.bfloat16),
                pltpu.VMEM((27 * CH, CH), jnp.bfloat16),
                pltpu.VMEM((OCT, BRICKS, EDGE, CH), jnp.float32),
                act_s,
                *norm_s,
                pltpu.SemaphoreType.DMA((3,)),
            ],
            compiler_params=pltpu.CompilerParams(vmem_limit_bytes=LIMIT),
            cost_estimate=pl.CostEstimate(flops=2 * 10**9, bytes_accessed=2**22, transcendentals=2**17),
            name=f"conv{step}",
        )(*inputs)
        if step < 3:
            act, sends = result[0], result[1:7]
            if step == 1:
                state = result[7]
    arrived = lax.all_to_all(result[0], "range", split_axis=0, concat_axis=0, tiled=True)
    slab = 32
    return pl.pallas_call(
        grow_kernel,
        grid=(128 // slab,),
        out_shape=bf16(128, OCT, 4 * CH),
        in_specs=[
            pl.BlockSpec((slab, OCT, CH), lambda i: (i, 0, 0)),
            pl.BlockSpec((CH, 4 * CH), lambda i: (0, 0)),
        ],
        out_specs=pl.BlockSpec((slab, OCT, 4 * CH), lambda i: (i, 0, 0)),
        compiler_params=pltpu.CompilerParams(vmem_limit_bytes=32 * 1024 * 1024),
        name="grow",
    )(arrived, up_weight)


def solution(mesh):
    split = P(("slab", "range"))
    return jax.shard_map(
        shards,
        mesh=mesh,
        in_specs=(split, split, split, split, P(), P(), P(), P()),
        out_specs=split,
        check_vma=False,
    )
```

```python
import functools

import jax
import jax.numpy as jnp
from jax import lax
from jax.experimental import pallas as pl
from jax.experimental.pallas import tpu as pltpu
from jax.sharding import PartitionSpec as P


EDGE = 8
CH = 128
BRICKS = 2
VOX = EDGE**3
OCT = 64
PITCH = 24
FACE = EDGE * EDGE
DIRECTIONS = [
    (dx, dy, dz)
    for dx in (-1, 0, 1)
    for dy in (-1, 0, 1)
    for dz in (-1, 0, 1)
    if (dx, dy, dz) != (0, 0, 0)
]
OWN_HI, OWN_LO, CORE, RANGE, SLAB_A, SLAB_B, ZERO = 0, 6, 12, 18, 24, 26, 28
FACES = 29

VMEM = pl.BlockSpec(memory_space=pltpu.VMEM)
SMEM = pl.BlockSpec(memory_space=pltpu.SMEM)
ANY = pl.BlockSpec(memory_space=pl.ANY)
HBM = pl.BlockSpec(memory_space=pltpu.HBM)


def group_sum(rows):
    lane = lax.broadcasted_iota(jnp.int32, rows.shape, 1)
    pair = jnp.where(lane % 2 == 0, pltpu.roll(rows, CH - 1, 1), pltpu.roll(rows, 1, 1))
    rows = rows + pair
    pair = jnp.where(lane % 4 < 2, pltpu.roll(rows, CH - 2, 1), pltpu.roll(rows, 2, 1))
    return jnp.sum(rows + pair, axis=0, keepdims=True)


def normalize(load, gain, shift):
    size = VOX * 4.0
    mean = group_sum(jnp.sum(load(), axis=0)) / size
    centred = load() - mean
    spread = group_sum(jnp.sum(centred * centred, axis=0)) / size
    scale = lax.rsqrt(spread + 1e-6) * gain
    w = (load() - mean) * scale + shift
    return w * (0.5 + 0.5 * jnp.tanh(0.5 * w))


def emit_active(load, b, gain, shift, act_s, act, sends):
    value = normalize(load, gain, shift)
    act_s[pl.ds(b * VOX, VOX)] = value.reshape(VOX, CH)
    act[b] = value.reshape(VOX, CH).astype(jnp.bfloat16)
    last, first, _, _, _, _ = sends
    base = b * VOX
    for x in range(EDGE):
        rows = pl.ds(x * EDGE, EDGE)
        for side, plane in ((7, last), (0, first)):
            plane[0, b, rows] = act_s[pl.ds(base + side * 64 + x * 8, 8)].astype(jnp.bfloat16)
            plane[1, b, rows] = act_s[pl.ds(base + x * 64 + side * 8, 8)].astype(jnp.bfloat16)
            plane[2, b, rows] = act_s[pl.ds(base + x * 64 + side, 8, stride=8)].astype(jnp.bfloat16)


def parity(axis):
    return lax.rem(lax.axis_index(axis), 2)


def choose_sends(sends):
    last, first, to_core, to_range, to_a, to_b = sends

    def route(flag, yes, no):
        @pl.when(flag == 0)
        def _():
            yes[...] = last[...] if yes.shape[0] == 3 else last[0]
            no[...] = first[...] if no.shape[0] == 3 else first[0]

        @pl.when(flag != 0)
        def _():
            yes[...] = first[...] if yes.shape[0] == 3 else first[0]
            no[...] = last[...] if no.shape[0] == 3 else last[0]

    route(parity("range"), to_core, to_range)
    route(parity("slab"), to_a, to_b)


def fetch(sems, *pairs):
    copies = [pltpu.make_async_copy(src, dst, sems.at[i]) for i, (src, dst) in enumerate(pairs)]
    for copy in copies:
        copy.start()
    return copies


def start_kernel(
    features_hbm, gain_hbm, shift_hbm, act, last, first, to_core, to_range, to_a, to_b,
    act_s, features, gain, shift, sems,
):
    copies = fetch(sems, (gain_hbm, gain), (shift_hbm, shift), *[(features_hbm.at[b], features.at[b]) for b in range(BRICKS)])
    for copy in copies[:2]:
        copy.wait()
    sends = (last, first, to_core, to_range, to_a, to_b)
    for b in range(BRICKS):
        copies[2 + b].wait()
        load = lambda b=b: features[b].astype(jnp.float32).reshape(OCT, EDGE, CH)
        emit_active(load, b, gain[0:1], shift[0:1], act_s, act, sends)
    choose_sends(sends)


def route_kernel(neighbours_hbm, kept_hbm, owner_hbm, after, faces, slots, neighbours, kept, owner, sems):
    for copy in fetch(sems, (neighbours_hbm, neighbours), (kept_hbm, kept), (owner_hbm, owner)):
        copy.wait()
    odd_range, odd_slab = parity("range"), parity("slab")
    below = jnp.where(odd_range == 1, CORE, RANGE)
    above = jnp.where(odd_range == 1, RANGE, CORE)
    under = jnp.where(odd_slab == 1, SLAB_A, SLAB_B)
    over = jnp.where(odd_slab == 1, SLAB_B, SLAB_A)
    for b in range(BRICKS):
        for k, offsets in enumerate(DIRECTIONS):
            axis = [a for a in range(3) if offsets[a] != 0][0]
            negative = offsets[axis] < 0
            entry = neighbours[b, k]
            source = entry // BRICKS
            own, side, slab = (OWN_HI, below, under) if negative else (OWN_LO, above, over)
            near = jnp.where(source == 0, own, side) + axis * BRICKS
            face = jnp.where(source > 2, slab, near) + entry % BRICKS
            face = jnp.where(entry < 0, ZERO, jnp.clip(face, 0, ZERO))
            faces[b, k] = face * FACE
    owners = [owner[c // 8, c % 8] for c in range(8 * BRICKS)]
    keeps = [kept[c // 8, c % 8] for c in range(8 * BRICKS)]
    for c in range(8 * BRICKS):
        rank = jnp.int32(0)
        for e in range(c):
            same = (owners[e] == owners[c]) & (keeps[e] == 1)
            rank = rank + jnp.where(same, 1, 0)
        slot = jnp.clip(owners[c] * 2 + jnp.minimum(rank, 1), 0, 127)
        slots[c] = jnp.where(keeps[c] == 1, slot, -1)


def gather_halos(faces, planes, table, field, halos):
    row = 0
    for plane in planes:
        whole = plane[...].astype(jnp.float32)
        count = whole.size // CH
        table[pl.ds(row, count)] = whole.reshape(count, CH)
        row += count
    table[pl.ds(ZERO * FACE, FACE)] = jnp.zeros((FACE, CH), jnp.float32)

    def cell(kind, side, i, b):
        return (((kind * 2 + side) * 10 + i) * BRICKS + b) * PITCH

    across = BRICKS * PITCH
    for side in range(2):
        for deep in (7, 16):
            field[pl.ds(cell(2, side, 1, 0) + deep, 16, stride=PITCH)] = jnp.zeros((16, CH), jnp.float32)
        for kind in (1, 2):
            for i in (0, 9):
                halos[kind, side, i] = jnp.zeros((BRICKS * EDGE, 3 * CH), jnp.bfloat16)
    for b in range(BRICKS):
        for k, (dx, dy, dz) in enumerate(DIRECTIONS):
            base = pl.multiple_of(faces[b, k], FACE)
            cut = lambda d: 7 if d < 0 else 0
            put = lambda d: 0 if d < 0 else 9
            deep = 7 if dz < 0 else 16
            kind = 0 if dx != 0 else 1 if dy != 0 else 2
            side = 0 if (dx, dy, dz)[kind] < 0 else 1
            if kind == 0 and dy != 0:
                there = cell(0, side, put(dy), b)
                if dz == 0:
                    field[pl.ds(there + 8, 8)] = table[pl.ds(base + cut(dy) * 8, 8)]
                else:
                    field[pl.ds(there + deep, 1)] = table[pl.ds(base + cut(dy) * 8 + cut(dz), 1)]
            elif kind < 2 and dz != 0:
                column = table[pl.ds(base + cut(dz), 8, stride=8)]
                field[pl.ds(cell(kind, side, 1, b) + deep, 8, stride=across)] = column
            else:
                for i in range(EDGE):
                    field[pl.ds(cell(kind, side, i + 1, b) + 8, 8)] = table[pl.ds(base + i * 8, 8)]
    for kind in range(3):
        for side in range(2):
            for i in range(10) if kind == 0 else range(1, 9):
                for w in range(3):
                    tile = jnp.concatenate(
                        [field[pl.ds(cell(kind, side, i, b) + 7 + w, 8)] for b in range(BRICKS)], axis=0
                    )
                    halos[kind, side, i, :, w * CH : (w + 1) * CH] = tile.astype(jnp.bfloat16)


def add_halos(halos, weights, acc):
    rows = EDGE * BRICKS * EDGE
    for kind in range(3):
        wide = jnp.concatenate([halos[kind, :, s : s + 8] for s in range(3)], axis=-1)
        sides = []
        for near in (0, 2):
            taps = []
            for s in range(3):
                for w in range(3):
                    tap = [(near * 3 + s) * 3 + w, (s * 3 + near) * 3 + w, (s * 3 + w) * 3 + near][kind]
                    taps.append(weights[pl.ds(tap * CH, CH)])
            sides.append(jnp.concatenate(taps, axis=0))
        part = jnp.dot(
            wide.reshape(2 * rows, 9 * CH), jnp.concatenate(sides, axis=1), preferred_element_type=jnp.float32
        )
        for side, edge in ((0, 0), (1, 7)):
            own = part[side * rows : (side + 1) * rows, side * CH : (side + 1) * CH]
            if kind == 0:
                acc[pl.ds(edge * rows, rows)] += own
                continue
            for x in range(EDGE):
                if kind == 1:
                    acc[pl.ds(x * rows + edge * 16, 16)] += own[x * 16 : x * 16 + 16]
                    continue
                for b in range(BRICKS):
                    line = pl.ds(x * rows + b * 8 + edge, 8, stride=16)
                    acc[line] = acc[line] + own[(x * 2 + b) * 8 : (x * 2 + b) * 8 + 8]


def convolve(window, weights, total):
    for p in range(3):
        rows = jnp.concatenate([window[p : p + 8, t : t + 8] for t in range(3)], axis=-1)
        part = jnp.dot(
            rows.reshape(BRICKS * VOX, 9 * CH),
            weights[p * 9 * CH : (p + 1) * 9 * CH],
            preferred_element_type=jnp.float32,
        ).reshape(OCT, BRICKS, EDGE, CH)
        if p == 0:
            total[...] = part
        else:
            total[...] += part


def inner_kernel(step, act, weights_hbm, total, weights, window, sems):
    copies = fetch(sems, (weights_hbm.at[step], weights))
    blank = jnp.zeros((BRICKS * EDGE, 3 * CH), jnp.bfloat16)
    row = lax.broadcasted_iota(jnp.int32, (EDGE, CH), 0)
    for x in range(10):
        for y in range(10):
            if not (0 < x < 9 and 0 < y < 9):
                window[x, y] = blank
                continue
            here = pl.ds(((x - 1) * 8 + y - 1) * 8, 8)
            tiles = [act[b, here].astype(jnp.float32) for b in range(BRICKS)]
            shifts = (
                [jnp.where(row > 0, pltpu.roll(t, 1, 0), 0.0) for t in tiles],
                tiles,
                [jnp.where(row < 7, pltpu.roll(t, 7, 0), 0.0) for t in tiles],
            )
            for w in range(3):
                window[x, y, :, w * CH : (w + 1) * CH] = jnp.concatenate(shifts[w], axis=0).astype(jnp.bfloat16)
    copies[0].wait()
    convolve(window, weights, total)


def conv_kernel(
    step, faces, last, first, core, rng, slab_a, slab_b, total, weights, gain_hbm, shift_hbm, *rest,
):
    rest = list(rest)
    state = rest.pop(0) if step % 2 else None
    slots = rest.pop(0) if step == 3 else None
    if step == 3:
        packed = rest.pop(0)
    else:
        act_out = rest.pop(0)
        sends = [rest.pop(0) for _ in range(6)]
        state_out = rest.pop(0) if step == 1 else None
    table, field, halos, acc, result, act_s, gain, shift, sems = rest
    copies = fetch(sems, (gain_hbm, gain), (shift_hbm, shift)) if step < 3 else []
    gather_halos(faces, (last, first, core, rng, slab_a, slab_b), table, field, halos)
    acc[...] = total[...].reshape(BRICKS * VOX, CH)
    add_halos(halos, weights, acc)
    if step == 3:
        packed[...] = jnp.zeros(packed.shape, packed.dtype)
    for copy in copies:
        copy.wait()
    for b in range(BRICKS):
        value = acc[...].reshape(OCT, BRICKS, EDGE, CH)[:, b]
        if step % 2:
            value = value + state[b].astype(jnp.float32).reshape(OCT, EDGE, CH)
        value = value.astype(jnp.bfloat16)
        if step == 1:
            state_out[b] = value.reshape(VOX, CH)
        result[b] = value.astype(jnp.float32)
        if step < 3:
            load = lambda b=b: result[b]
            emit_active(load, b, gain[step + 1 : step + 2], shift[step + 1 : step + 2], act_s, act_out, sends)
    if step < 3:
        choose_sends(sends)
        return
    low = lax.broadcasted_iota(jnp.int32, (4, 2, 8, CH), 2) < 4
    for b in range(BRICKS):
        for ox in range(2):
            for oy in range(2):
                tiles = result[b, pl.ds(ox * 32, 32)].reshape(4, 8, EDGE, CH)
                tiles = tiles[:, oy * 4 : oy * 4 + 4].reshape(4, 2, 2, EDGE, CH)
                even, odd = tiles[:, :, 0], tiles[:, :, 1]
                turn = lambda v: pltpu.roll(v.reshape(8, EDGE, CH), 4, 1).reshape(4, 2, EDGE, CH)
                for oz in range(2):
                    block = jnp.where(low, even, turn(odd)) if oz == 0 else jnp.where(low, turn(even), odd)
                    child = b * 8 + (ox * 2 + oy) * 2 + oz
                    block = block.reshape(OCT, CH).astype(jnp.bfloat16)
                    slot = slots[child]

                    @pl.when(slot >= 0)
                    def _(slot=slot, block=block):
                        packed[slot] = block


def grow_kernel(octants, up, out):
    rows = octants[...].reshape(-1, CH)
    grown = jnp.dot(rows, up[...], preferred_element_type=jnp.float32)
    out[...] = grown.astype(jnp.bfloat16).reshape(out.shape)


def bf16(*shape):
    return jax.ShapeDtypeStruct(shape, jnp.bfloat16)


def swap(block, axis, odd):
    count = lax.axis_size(axis)
    route = []
    for i in range(count):
        j = (i ^ 1) if not odd else (i + 1 if i % 2 else i - 1)
        route.append((i, j % count))
    return lax.ppermute(block, axis, route)


def exchange(sends):
    last, first, to_core, to_range, to_a, to_b = sends
    rng = swap(to_range, "range", True)
    slab_b = swap(to_b, "slab", True)
    slab_a = swap(to_a, "slab", False)
    core = swap(to_core, "range", False)
    return last, first, core, rng, slab_a, slab_b


SENDS = [
    bf16(3, BRICKS, FACE, CH),
    bf16(3, BRICKS, FACE, CH),
    bf16(3, BRICKS, FACE, CH),
    bf16(3, BRICKS, FACE, CH),
    bf16(BRICKS, FACE, CH),
    bf16(BRICKS, FACE, CH),
]
LIMIT = 16 * 1024 * 1024


def shards(features, neighbours, keep_mask, owner, norm_gain, norm_shift, conv_weights, up_weight):
    act_s = pltpu.VMEM((BRICKS * VOX, CH), jnp.float32)
    norm_s = [pltpu.VMEM((4, CH), jnp.float32)] * 2
    in_hbm = lambda v: pltpu.with_memory_space_constraint(v, pltpu.HBM)
    gain, shift = in_hbm(norm_gain), in_hbm(norm_shift)
    act, *sends = pl.pallas_call(
        start_kernel,
        out_shape=[bf16(BRICKS, VOX, CH), *SENDS],
        in_specs=[HBM] * 3,
        out_specs=[VMEM] * 7,
        scratch_shapes=[
            act_s,
            pltpu.VMEM((BRICKS, VOX, CH), jnp.bfloat16),
            *norm_s,
            pltpu.SemaphoreType.DMA((2 + BRICKS,)),
        ],
        compiler_params=pltpu.CompilerParams(vmem_limit_bytes=LIMIT),
        cost_estimate=pl.CostEstimate(flops=10**7, bytes_accessed=2**22, transcendentals=2**17),
        name="start",
    )(in_hbm(features), gain, shift)
    faces, slots = pl.pallas_call(
        route_kernel,
        out_shape=[jax.ShapeDtypeStruct((BRICKS, 26), jnp.int32), jax.ShapeDtypeStruct((8 * BRICKS,), jnp.int32)],
        in_specs=[HBM, HBM, HBM, ANY],
        out_specs=[SMEM, SMEM],
        scratch_shapes=[
            pltpu.SMEM((BRICKS, 26), jnp.int32),
            pltpu.SMEM((BRICKS, 8), jnp.int32),
            pltpu.SMEM((BRICKS, 8), jnp.int32),
            pltpu.SemaphoreType.DMA((3,)),
        ],
        compiler_params=pltpu.CompilerParams(vmem_limit_bytes=LIMIT),
        cost_estimate=pl.CostEstimate(flops=1000, bytes_accessed=4096, transcendentals=0),
        name="route",
    )(in_hbm(neighbours), in_hbm(keep_mask), in_hbm(owner), act)
    all_weights = in_hbm(conv_weights.reshape(4, 27 * CH, CH))
    state = features
    for step in range(4):
        planes = exchange(sends)
        total, weights = pl.pallas_call(
            functools.partial(inner_kernel, step),
            out_shape=[jax.ShapeDtypeStruct((OCT, BRICKS, EDGE, CH), jnp.float32), bf16(27 * CH, CH)],
            in_specs=[VMEM, HBM],
            out_specs=[VMEM, VMEM],
            scratch_shapes=[
                pltpu.VMEM((10, 10, BRICKS * EDGE, 3 * CH), jnp.bfloat16),
                pltpu.SemaphoreType.DMA((1,)),
            ],
            compiler_params=pltpu.CompilerParams(vmem_limit_bytes=LIMIT),
            cost_estimate=pl.CostEstimate(flops=2 * 10**9, bytes_accessed=2**21, transcendentals=0),
        )(act, all_weights)
        inputs = [faces, *planes, total, weights, gain, shift]
        in_specs = [SMEM] + [VMEM] * 8 + [HBM] * 2
        if step % 2:
            inputs.append(state)
            in_specs.append(VMEM)
        if step == 3:
            inputs.append(slots)
            in_specs.append(SMEM)
            outs = [bf16(128, OCT, CH)]
        else:
            outs = [bf16(BRICKS, VOX, CH), *SENDS]
            if step == 1:
                outs.append(bf16(BRICKS, VOX, CH))
        result = pl.pallas_call(
            functools.partial(conv_kernel, step),
            out_shape=outs,
            in_specs=in_specs,
            out_specs=[VMEM] * len(outs),
            scratch_shapes=[
                pltpu.VMEM((FACES * FACE, CH), jnp.float32),
                pltpu.VMEM((6 * 10 * BRICKS * PITCH, CH), jnp.float32),
                pltpu.VMEM((3, 2, 10, BRICKS * EDGE, 3 * CH), jnp.bfloat16),
                pltpu.VMEM((BRICKS * VOX, CH), jnp.float32),
                pltpu.VMEM((BRICKS, OCT, EDGE, CH), jnp.float32),
                act_s,
                *norm_s,
                pltpu.SemaphoreType.DMA((2,)),
            ],
            compiler_params=pltpu.CompilerParams(vmem_limit_bytes=LIMIT),
            cost_estimate=pl.CostEstimate(flops=5 * 10**8, bytes_accessed=2**22, transcendentals=2**17),
        )(*inputs)
        if step < 3:
            act, sends = result[0], result[1:7]
            if step == 1:
                state = result[7]
    arrived = lax.all_to_all(result[0], "range", split_axis=0, concat_axis=0, tiled=True)
    slab = 32
    return pl.pallas_call(
        grow_kernel,
        grid=(128 // slab,),
        out_shape=bf16(128, OCT, 4 * CH),
        in_specs=[
            pl.BlockSpec((slab, OCT, CH), lambda i: (i, 0, 0)),
            pl.BlockSpec((CH, 4 * CH), lambda i: (0, 0)),
        ],
        out_specs=pl.BlockSpec((slab, OCT, 4 * CH), lambda i: (i, 0, 0)),
        compiler_params=pltpu.CompilerParams(vmem_limit_bytes=32 * 1024 * 1024),
        name="grow",
    )(arrived, up_weight)


def solution(mesh):
    split = P(("slab", "range"))
    return jax.shard_map(
        shards,
        mesh=mesh,
        in_specs=(split, split, split, split, P(), P(), P(), P()),
        out_specs=split,
        check_vma=False,
    )
```

```python
import functools

import jax
import jax.numpy as jnp
from jax import lax
from jax.experimental import pallas as pl
from jax.experimental.pallas import tpu as pltpu
from jax.sharding import PartitionSpec as P


EDGE = 8
CH = 128
BRICKS = 2
VOX = EDGE**3
OCT = 64
PITCH = 24
FACE = EDGE * EDGE
DIRECTIONS = [
    (dx, dy, dz)
    for dx in (-1, 0, 1)
    for dy in (-1, 0, 1)
    for dz in (-1, 0, 1)
    if (dx, dy, dz) != (0, 0, 0)
]
OWN_HI, OWN_LO, CORE, RANGE, SLAB_A, SLAB_B, ZERO = 0, 6, 12, 18, 24, 26, 28
FACES = 29

VMEM = pl.BlockSpec(memory_space=pltpu.VMEM)
SMEM = pl.BlockSpec(memory_space=pltpu.SMEM)
HBM = pl.BlockSpec(memory_space=pltpu.HBM)


def group_sum(rows):
    lane = lax.broadcasted_iota(jnp.int32, rows.shape, 1)
    pair = jnp.where(lane % 2 == 0, pltpu.roll(rows, CH - 1, 1), pltpu.roll(rows, 1, 1))
    rows = rows + pair
    pair = jnp.where(lane % 4 < 2, pltpu.roll(rows, CH - 2, 1), pltpu.roll(rows, 2, 1))
    return jnp.sum(rows + pair, axis=0, keepdims=True)


def normalize(load, gain, shift):
    size = VOX * 4.0
    mean = group_sum(jnp.sum(load(), axis=0)) / size
    centred = load() - mean
    spread = group_sum(jnp.sum(centred * centred, axis=0)) / size
    scale = lax.rsqrt(spread + 1e-6) * gain
    w = (load() - mean) * scale + shift
    return w * (0.5 + 0.5 * jnp.tanh(0.5 * w))


def emit_active(load, b, gain, shift, act_s, act, sends):
    value = normalize(load, gain, shift)
    act_s[pl.ds(b * VOX, VOX)] = value.reshape(VOX, CH)
    act[b] = value.reshape(VOX, CH).astype(jnp.bfloat16)
    last, first, _, _, _, _ = sends
    base = b * VOX
    for x in range(EDGE):
        rows = pl.ds(x * EDGE, EDGE)
        for side, plane in ((7, last), (0, first)):
            plane[0, b, rows] = act_s[pl.ds(base + side * 64 + x * 8, 8)].astype(jnp.bfloat16)
            plane[1, b, rows] = act_s[pl.ds(base + x * 64 + side * 8, 8)].astype(jnp.bfloat16)
            plane[2, b, rows] = act_s[pl.ds(base + x * 64 + side, 8, stride=8)].astype(jnp.bfloat16)


def parity(axis):
    return lax.rem(lax.axis_index(axis), 2)


def choose_sends(sends):
    last, first, to_core, to_range, to_a, to_b = sends

    def route(flag, yes, no):
        @pl.when(flag == 0)
        def _():
            yes[...] = last[...] if yes.shape[0] == 3 else last[0]
            no[...] = first[...] if no.shape[0] == 3 else first[0]

        @pl.when(flag != 0)
        def _():
            yes[...] = first[...] if yes.shape[0] == 3 else first[0]
            no[...] = last[...] if no.shape[0] == 3 else last[0]

    route(parity("range"), to_core, to_range)
    route(parity("slab"), to_a, to_b)


def fetch(sems, *pairs):
    copies = [pltpu.make_async_copy(src, dst, sems.at[i]) for i, (src, dst) in enumerate(pairs)]
    for copy in copies:
        copy.start()
    return copies


def start_kernel(
    features_hbm, gain_hbm, shift_hbm, act, last, first, to_core, to_range, to_a, to_b,
    act_s, features, gain, shift, sems,
):
    copies = fetch(sems, (gain_hbm, gain), (shift_hbm, shift), *[(features_hbm.at[b], features.at[b]) for b in range(BRICKS)])
    for copy in copies[:2]:
        copy.wait()
    sends = (last, first, to_core, to_range, to_a, to_b)
    for b in range(BRICKS):
        copies[2 + b].wait()
        load = lambda b=b: features[b].astype(jnp.float32).reshape(OCT, EDGE, CH)
        emit_active(load, b, gain[0:1], shift[0:1], act_s, act, sends)
    choose_sends(sends)


def find_routes(neighbours, kept, owner, faces, slots):
    odd_range, odd_slab = parity("range"), parity("slab")
    below = jnp.where(odd_range == 1, CORE, RANGE)
    above = jnp.where(odd_range == 1, RANGE, CORE)
    under = jnp.where(odd_slab == 1, SLAB_A, SLAB_B)
    over = jnp.where(odd_slab == 1, SLAB_B, SLAB_A)
    for b in range(BRICKS):
        for k, offsets in enumerate(DIRECTIONS):
            axis = [a for a in range(3) if offsets[a] != 0][0]
            negative = offsets[axis] < 0
            entry = neighbours[b, k]
            source = entry >> 1
            own, side, slab = (OWN_HI, below, under) if negative else (OWN_LO, above, over)
            near = jnp.where(source == 0, own, side) + axis * BRICKS
            face = jnp.where(source > 2, slab, near) + (entry & 1)
            face = jnp.where(entry < 0, ZERO, jnp.clip(face, 0, ZERO))
            faces[b, k] = face * FACE
    owners = [owner[c // 8, c % 8] for c in range(8 * BRICKS)]
    keeps = [kept[c // 8, c % 8] for c in range(8 * BRICKS)]
    for c in range(8 * BRICKS):
        rank = jnp.int32(0)
        for e in range(c):
            same = (owners[e] == owners[c]) & (keeps[e] == 1)
            rank = rank + jnp.where(same, 1, 0)
        slot = jnp.clip(owners[c] * 2 + jnp.minimum(rank, 1), 0, 127)
        slots[c] = jnp.where(keeps[c] == 1, slot, -1)


def gather_halos(faces, planes, table, field, halos):
    row = 0
    for plane in planes:
        whole = plane[...].astype(jnp.float32)
        count = whole.size // CH
        table[pl.ds(row, count)] = whole.reshape(count, CH)
        row += count
    table[pl.ds(ZERO * FACE, FACE)] = jnp.zeros((FACE, CH), jnp.float32)

    def cell(kind, side, i, b):
        return (((kind * 2 + side) * 10 + i) * BRICKS + b) * PITCH

    across = BRICKS * PITCH
    for side in range(2):
        for deep in (7, 16):
            field[pl.ds(cell(2, side, 1, 0) + deep, 16, stride=PITCH)] = jnp.zeros((16, CH), jnp.float32)
        for kind in (1, 2):
            for i in (0, 9):
                halos[kind, side, i] = jnp.zeros((BRICKS * EDGE, 3 * CH), jnp.bfloat16)
    for b in range(BRICKS):
        for k, (dx, dy, dz) in enumerate(DIRECTIONS):
            base = pl.multiple_of(faces[b, k], FACE)
            cut = lambda d: 7 if d < 0 else 0
            put = lambda d: 0 if d < 0 else 9
            deep = 7 if dz < 0 else 16
            kind = 0 if dx != 0 else 1 if dy != 0 else 2
            side = 0 if (dx, dy, dz)[kind] < 0 else 1
            if kind == 0 and dy != 0:
                there = cell(0, side, put(dy), b)
                if dz == 0:
                    field[pl.ds(there + 8, 8)] = table[pl.ds(base + cut(dy) * 8, 8)]
                else:
                    field[pl.ds(there + deep, 1)] = table[pl.ds(base + cut(dy) * 8 + cut(dz), 1)]
            elif kind < 2 and dz != 0:
                column = table[pl.ds(base + cut(dz), 8, stride=8)]
                field[pl.ds(cell(kind, side, 1, b) + deep, 8, stride=across)] = column
            else:
                for i in range(EDGE):
                    field[pl.ds(cell(kind, side, i + 1, b) + 8, 8)] = table[pl.ds(base + i * 8, 8)]
    for kind in range(3):
        for side in range(2):
            for i in range(10) if kind == 0 else range(1, 9):
                for w in range(3):
                    tile = jnp.concatenate(
                        [field[pl.ds(cell(kind, side, i, b) + 7 + w, 8)] for b in range(BRICKS)], axis=0
                    )
                    halos[kind, side, i, :, w * CH : (w + 1) * CH] = tile.astype(jnp.bfloat16)


def add_halos(halos, weights, acc):
    rows = EDGE * BRICKS * EDGE
    for kind in range(3):
        wide = jnp.concatenate([halos[kind, :, s : s + 8] for s in range(3)], axis=-1)
        sides = []
        for near in (0, 2):
            taps = []
            for s in range(3):
                for w in range(3):
                    tap = [(near * 3 + s) * 3 + w, (s * 3 + near) * 3 + w, (s * 3 + w) * 3 + near][kind]
                    taps.append(weights[pl.ds(tap * CH, CH)])
            sides.append(jnp.concatenate(taps, axis=0))
        part = jnp.dot(
            wide.reshape(2 * rows, 9 * CH), jnp.concatenate(sides, axis=1), preferred_element_type=jnp.float32
        )
        for side, edge in ((0, 0), (1, 7)):
            own = part[side * rows : (side + 1) * rows, side * CH : (side + 1) * CH]
            if kind == 0:
                acc[pl.ds(edge * rows, rows)] += own
                continue
            for x in range(EDGE):
                if kind == 1:
                    acc[pl.ds(x * rows + edge * 16, 16)] += own[x * 16 : x * 16 + 16]
                    continue
                for b in range(BRICKS):
                    line = pl.ds(x * rows + b * 8 + edge, 8, stride=16)
                    acc[line] = acc[line] + own[(x * 2 + b) * 8 : (x * 2 + b) * 8 + 8]


def convolve(window, weights, wide, total):
    rows = jnp.concatenate([window[p : p + 8] for p in range(3)], axis=-1).reshape(BRICKS * VOX, 9 * CH)
    taps = [
        jnp.concatenate([weights[pl.ds((p * 3 + t) * 3 * CH, 3 * CH)] for p in range(3)], axis=0) for t in range(3)
    ]
    wide[...] = jnp.dot(rows, jnp.concatenate(taps, axis=1), preferred_element_type=jnp.float32)
    line = BRICKS * EDGE
    for x in range(EDGE):
        for y in range(EDGE):
            here = (x * EDGE + y) * line
            value = wide[pl.ds(here, line), CH : 2 * CH]
            if y > 0:
                value = value + wide[pl.ds(here - line, line), :CH]
            if y < 7:
                value = value + wide[pl.ds(here + line, line), 2 * CH :]
            total[x * EDGE + y] = value.reshape(BRICKS, EDGE, CH)


def inner_kernel(step, act, weights_src, *rest):
    if step == 0:
        *tables_hbm, total, weights, faces, slots, window, wide, neighbours, kept, owner, sems = rest
        tables = (neighbours, kept, owner)
        copies = fetch(sems, (weights_src.at[0], weights), *zip(tables_hbm, tables))
        for copy in copies[1:]:
            copy.wait()
        find_routes(*tables, faces, slots)
    else:
        total, window, wide = rest
        weights = weights_src.at[step]
    blank = jnp.zeros((BRICKS * EDGE, 3 * CH), jnp.bfloat16)
    row = lax.broadcasted_iota(jnp.int32, (EDGE, CH), 0)
    for x in range(10):
        for y in range(8):
            if not 0 < x < 9:
                window[x, y] = blank
                continue
            here = pl.ds(((x - 1) * 8 + y) * 8, 8)
            tiles = [act[b, here].astype(jnp.float32) for b in range(BRICKS)]
            shifts = (
                [jnp.where(row > 0, pltpu.roll(t, 1, 0), 0.0) for t in tiles],
                tiles,
                [jnp.where(row < 7, pltpu.roll(t, 7, 0), 0.0) for t in tiles],
            )
            for w in range(3):
                window[x, y, :, w * CH : (w + 1) * CH] = jnp.concatenate(shifts[w], axis=0).astype(jnp.bfloat16)
    if step == 0:
        copies[0].wait()
    convolve(window, weights, wide, total)


def conv_kernel(
    step, faces, last, first, core, rng, slab_a, slab_b, total, weights, gain_hbm, shift_hbm, *rest,
):
    rest = list(rest)
    state = rest.pop(0) if step % 2 else None
    slots = rest.pop(0) if step == 3 else None
    if step == 3:
        packed = rest.pop(0)
    else:
        act_out = rest.pop(0)
        sends = [rest.pop(0) for _ in range(6)]
        state_out = rest.pop(0) if step == 1 else None
    table, field, halos, acc, result, act_s, gain, shift, sems = rest
    copies = fetch(sems, (gain_hbm, gain), (shift_hbm, shift)) if step < 3 else []
    gather_halos(faces, (last, first, core, rng, slab_a, slab_b), table, field, halos)
    acc[...] = total[...].reshape(BRICKS * VOX, CH)
    add_halos(halos, weights.at[step] if step else weights, acc)
    if step == 3:
        packed[...] = jnp.zeros(packed.shape, packed.dtype)
    for copy in copies:
        copy.wait()
    for b in range(BRICKS):
        value = acc[...].reshape(OCT, BRICKS, EDGE, CH)[:, b]
        if step % 2:
            value = value + state[b].astype(jnp.float32).reshape(OCT, EDGE, CH)
        value = value.astype(jnp.bfloat16)
        if step == 1:
            state_out[b] = value.reshape(VOX, CH)
        result[b] = value.astype(jnp.float32)
        if step < 3:
            load = lambda b=b: result[b]
            emit_active(load, b, gain[step + 1 : step + 2], shift[step + 1 : step + 2], act_s, act_out, sends)
    if step < 3:
        choose_sends(sends)
        return
    low = lax.broadcasted_iota(jnp.int32, (4, 2, 8, CH), 2) < 4
    for b in range(BRICKS):
        for ox in range(2):
            for oy in range(2):
                tiles = result[b, pl.ds(ox * 32, 32)].reshape(4, 8, EDGE, CH)
                tiles = tiles[:, oy * 4 : oy * 4 + 4].reshape(4, 2, 2, EDGE, CH)
                even, odd = tiles[:, :, 0], tiles[:, :, 1]
                turn = lambda v: pltpu.roll(v.reshape(8, EDGE, CH), 4, 1).reshape(4, 2, EDGE, CH)
                for oz in range(2):
                    block = jnp.where(low, even, turn(odd)) if oz == 0 else jnp.where(low, turn(even), odd)
                    child = b * 8 + (ox * 2 + oy) * 2 + oz
                    block = block.reshape(OCT, CH).astype(jnp.bfloat16)
                    slot = slots[child]

                    @pl.when(slot >= 0)
                    def _(slot=slot, block=block):
                        packed[slot] = block


def grow_kernel(octants, up, out, grown, sems):
    copies = []
    for i in range(PARTS):
        part = pl.ds(i * (128 // PARTS), 128 // PARTS)
        rows = octants[part].reshape(-1, CH)
        value = jnp.dot(rows, up[...], preferred_element_type=jnp.float32)
        grown[part] = value.astype(jnp.bfloat16).reshape(128 // PARTS, OCT, 4 * CH)
        copies.append(pltpu.make_async_copy(grown.at[part], out.at[part], sems.at[i]))
        copies[-1].start()
    for copy in copies:
        copy.wait()


def bf16(*shape):
    return jax.ShapeDtypeStruct(shape, jnp.bfloat16)


def swap(block, axis, odd):
    count = lax.axis_size(axis)
    route = []
    for i in range(count):
        j = (i ^ 1) if not odd else (i + 1 if i % 2 else i - 1)
        route.append((i, j % count))
    return lax.ppermute(block, axis, route)


def exchange(sends):
    last, first, to_core, to_range, to_a, to_b = sends
    rng = swap(to_range, "range", True)
    slab_b = swap(to_b, "slab", True)
    slab_a = swap(to_a, "slab", False)
    core = swap(to_core, "range", False)
    return last, first, core, rng, slab_a, slab_b


SENDS = [
    bf16(3, BRICKS, FACE, CH),
    bf16(3, BRICKS, FACE, CH),
    bf16(3, BRICKS, FACE, CH),
    bf16(3, BRICKS, FACE, CH),
    bf16(BRICKS, FACE, CH),
    bf16(BRICKS, FACE, CH),
]
LIMIT = 16 * 1024 * 1024
PARTS = 16


def shards(features, neighbours, keep_mask, owner, norm_gain, norm_shift, conv_weights, up_weight):
    act_s = pltpu.VMEM((BRICKS * VOX, CH), jnp.float32)
    norm_s = [pltpu.VMEM((4, CH), jnp.float32)] * 2
    in_hbm = lambda v: pltpu.with_memory_space_constraint(v, pltpu.HBM)
    gain, shift = in_hbm(norm_gain), in_hbm(norm_shift)
    act, *sends = pl.pallas_call(
        start_kernel,
        out_shape=[bf16(BRICKS, VOX, CH), *SENDS],
        in_specs=[HBM] * 3,
        out_specs=[VMEM] * 7,
        scratch_shapes=[
            act_s,
            pltpu.VMEM((BRICKS, VOX, CH), jnp.bfloat16),
            *norm_s,
            pltpu.SemaphoreType.DMA((2 + BRICKS,)),
        ],
        compiler_params=pltpu.CompilerParams(vmem_limit_bytes=LIMIT),
        cost_estimate=pl.CostEstimate(flops=10**7, bytes_accessed=2**22, transcendentals=2**17),
        name="start",
    )(in_hbm(features), gain, shift)
    all_weights = conv_weights.reshape(4, 27 * CH, CH)
    state = features
    for step in range(4):
        planes = exchange(sends)
        window_s = [
            pltpu.VMEM((10, 8, BRICKS * EDGE, 3 * CH), jnp.bfloat16),
            pltpu.VMEM((BRICKS * VOX, 3 * CH), jnp.float32),
        ]
        call = functools.partial(
            pl.pallas_call,
            functools.partial(inner_kernel, step),
            compiler_params=pltpu.CompilerParams(vmem_limit_bytes=LIMIT),
            cost_estimate=pl.CostEstimate(flops=2 * 10**9, bytes_accessed=2**21, transcendentals=0),
        )
        total_t = jax.ShapeDtypeStruct((OCT, BRICKS, EDGE, CH), jnp.float32)
        if step == 0:
            total, weights, faces, slots = call(
                out_shape=[
                    total_t,
                    bf16(27 * CH, CH),
                    jax.ShapeDtypeStruct((BRICKS, 26), jnp.int32),
                    jax.ShapeDtypeStruct((8 * BRICKS,), jnp.int32),
                ],
                in_specs=[VMEM] + [HBM] * 4,
                out_specs=[VMEM, VMEM, SMEM, SMEM],
                scratch_shapes=[
                    *window_s,
                    pltpu.SMEM((BRICKS, 26), jnp.int32),
                    pltpu.SMEM((BRICKS, 8), jnp.int32),
                    pltpu.SMEM((BRICKS, 8), jnp.int32),
                    pltpu.SemaphoreType.DMA((4,)),
                ],
            )(act, in_hbm(all_weights), in_hbm(neighbours), in_hbm(keep_mask), in_hbm(owner))
        else:
            weights = all_weights
            (total,) = call(
                out_shape=[total_t], in_specs=[VMEM, VMEM], out_specs=[VMEM], scratch_shapes=window_s
            )(act, weights)
        inputs = [faces, *planes, total, weights, gain, shift]
        in_specs = [SMEM] + [VMEM] * 8 + [HBM] * 2
        if step % 2:
            inputs.append(state)
            in_specs.append(VMEM)
        if step == 3:
            inputs.append(slots)
            in_specs.append(SMEM)
            outs = [bf16(128, OCT, CH)]
        else:
            outs = [bf16(BRICKS, VOX, CH), *SENDS]
            if step == 1:
                outs.append(bf16(BRICKS, VOX, CH))
        result = pl.pallas_call(
            functools.partial(conv_kernel, step),
            out_shape=outs,
            in_specs=in_specs,
            out_specs=[VMEM] * len(outs),
            scratch_shapes=[
                pltpu.VMEM((FACES * FACE, CH), jnp.float32),
                pltpu.VMEM((6 * 10 * BRICKS * PITCH, CH), jnp.float32),
                pltpu.VMEM((3, 2, 10, BRICKS * EDGE, 3 * CH), jnp.bfloat16),
                pltpu.VMEM((BRICKS * VOX, CH), jnp.float32),
                pltpu.VMEM((BRICKS, OCT, EDGE, CH), jnp.float32),
                act_s,
                *norm_s,
                pltpu.SemaphoreType.DMA((2,)),
            ],
            compiler_params=pltpu.CompilerParams(vmem_limit_bytes=LIMIT),
            cost_estimate=pl.CostEstimate(flops=5 * 10**8, bytes_accessed=2**22, transcendentals=2**17),
        )(*inputs)
        if step < 3:
            act, sends = result[0], result[1:7]
            if step == 1:
                state = result[7]
    arrived = lax.all_to_all(result[0], "range", split_axis=0, concat_axis=0, tiled=True)
    return pl.pallas_call(
        grow_kernel,
        out_shape=bf16(128, OCT, 4 * CH),
        in_specs=[VMEM, VMEM],
        out_specs=HBM,
        scratch_shapes=[pltpu.VMEM((128, OCT, 4 * CH), jnp.bfloat16), pltpu.SemaphoreType.DMA((PARTS,))],
        compiler_params=pltpu.CompilerParams(vmem_limit_bytes=32 * 1024 * 1024),
        name="grow",
    )(arrived, up_weight)


def solution(mesh):
    split = P(("slab", "range"))
    return jax.shard_map(
        shards,
        mesh=mesh,
        in_specs=(split, split, split, split, P(), P(), P(), P()),
        out_specs=split,
        check_vma=False,
    )
```

```python
import functools

import jax
import jax.numpy as jnp
from jax import lax
from jax.experimental import pallas as pl
from jax.experimental.pallas import tpu as pltpu
from jax.sharding import PartitionSpec as P


EDGE = 8
CH = 128
BRICKS = 2
VOX = EDGE**3
OCT = 64
PITCH = 24
FACE = EDGE * EDGE
DIRECTIONS = [
    (dx, dy, dz)
    for dx in (-1, 0, 1)
    for dy in (-1, 0, 1)
    for dz in (-1, 0, 1)
    if (dx, dy, dz) != (0, 0, 0)
]
OWN_HI, OWN_LO, CORE, RANGE, SLAB_A, SLAB_B, ZERO = 0, 6, 12, 18, 24, 26, 28
FACES = 29

VMEM = pl.BlockSpec(memory_space=pltpu.VMEM)
SMEM = pl.BlockSpec(memory_space=pltpu.SMEM)
HBM = pl.BlockSpec(memory_space=pltpu.HBM)


def group_sum(rows):
    lane = lax.broadcasted_iota(jnp.int32, rows.shape, 1)
    pair = jnp.where(lane % 2 == 0, pltpu.roll(rows, CH - 1, 1), pltpu.roll(rows, 1, 1))
    rows = rows + pair
    pair = jnp.where(lane % 4 < 2, pltpu.roll(rows, CH - 2, 1), pltpu.roll(rows, 2, 1))
    return jnp.sum(rows + pair, axis=0, keepdims=True)


def normalize(load, gain, shift):
    size = VOX * 4.0
    mean = group_sum(jnp.sum(load(), axis=0)) / size
    centred = load() - mean
    spread = group_sum(jnp.sum(centred * centred, axis=0)) / size
    scale = lax.rsqrt(spread + 1e-6) * gain
    w = (load() - mean) * scale + shift
    return w * (0.5 + 0.5 * jnp.tanh(0.5 * w))


def emit_active(load, b, gain, shift, act_s, act, sends):
    value = normalize(load, gain, shift)
    act_s[pl.ds(b * VOX, VOX)] = value.reshape(VOX, CH)
    act[b] = value.reshape(VOX, CH).astype(jnp.bfloat16)
    last, first, _, _, _, _ = sends
    base = b * VOX
    for x in range(EDGE):
        rows = pl.ds(x * EDGE, EDGE)
        for side, plane in ((7, last), (0, first)):
            plane[0, b, rows] = act_s[pl.ds(base + side * 64 + x * 8, 8)].astype(jnp.bfloat16)
            plane[1, b, rows] = act_s[pl.ds(base + x * 64 + side * 8, 8)].astype(jnp.bfloat16)
            plane[2, b, rows] = act_s[pl.ds(base + x * 64 + side, 8, stride=8)].astype(jnp.bfloat16)


def parity(axis):
    return lax.rem(lax.axis_index(axis), 2)


def choose_sends(sends):
    last, first, to_core, to_range, to_a, to_b = sends

    def route(flag, yes, no):
        @pl.when(flag == 0)
        def _():
            yes[...] = last[...] if yes.shape[0] == 3 else last[0]
            no[...] = first[...] if no.shape[0] == 3 else first[0]

        @pl.when(flag != 0)
        def _():
            yes[...] = first[...] if yes.shape[0] == 3 else first[0]
            no[...] = last[...] if no.shape[0] == 3 else last[0]

    route(parity("range"), to_core, to_range)
    route(parity("slab"), to_a, to_b)


def fetch(sems, *pairs):
    copies = [pltpu.make_async_copy(src, dst, sems.at[i]) for i, (src, dst) in enumerate(pairs)]
    for copy in copies:
        copy.start()
    return copies


def start_kernel(
    features_hbm, gain_hbm, shift_hbm, act, last, first, to_core, to_range, to_a, to_b,
    act_s, features, gain, shift, sems,
):
    copies = fetch(sems, (gain_hbm, gain), (shift_hbm, shift), *[(features_hbm.at[b], features.at[b]) for b in range(BRICKS)])
    for copy in copies[:2]:
        copy.wait()
    sends = (last, first, to_core, to_range, to_a, to_b)
    for b in range(BRICKS):
        copies[2 + b].wait()
        load = lambda b=b: features[b].astype(jnp.float32).reshape(OCT, EDGE, CH)
        emit_active(load, b, gain[0:1], shift[0:1], act_s, act, sends)
    choose_sends(sends)


def find_routes(neighbours, kept, owner, faces, slots):
    odd_range, odd_slab = parity("range"), parity("slab")
    below = jnp.where(odd_range == 1, CORE, RANGE)
    above = jnp.where(odd_range == 1, RANGE, CORE)
    under = jnp.where(odd_slab == 1, SLAB_A, SLAB_B)
    over = jnp.where(odd_slab == 1, SLAB_B, SLAB_A)
    for b in range(BRICKS):
        for k, offsets in enumerate(DIRECTIONS):
            axis = [a for a in range(3) if offsets[a] != 0][0]
            negative = offsets[axis] < 0
            entry = neighbours[b, k]
            source = entry >> 1
            own, side, slab = (OWN_HI, below, under) if negative else (OWN_LO, above, over)
            near = jnp.where(source == 0, own, side) + axis * BRICKS
            face = jnp.where(source > 2, slab, near) + (entry & 1)
            face = jnp.where(entry < 0, ZERO, jnp.clip(face, 0, ZERO))
            faces[b, k] = face * FACE
    owners = [owner[c // 8, c % 8] for c in range(8 * BRICKS)]
    keeps = [kept[c // 8, c % 8] for c in range(8 * BRICKS)]
    for c in range(8 * BRICKS):
        rank = jnp.int32(0)
        for e in range(c):
            same = (owners[e] == owners[c]) & (keeps[e] == 1)
            rank = rank + jnp.where(same, 1, 0)
        slot = jnp.clip(owners[c] * 2 + jnp.minimum(rank, 1), 0, 127)
        slots[c] = jnp.where(keeps[c] == 1, slot, -1)


def gather_halos(faces, planes, table, field, halos):
    row = 0
    for plane in planes:
        whole = plane[...].astype(jnp.float32)
        count = whole.size // CH
        table[pl.ds(row, count)] = whole.reshape(count, CH)
        row += count
    table[pl.ds(ZERO * FACE, FACE)] = jnp.zeros((FACE, CH), jnp.float32)

    def cell(kind, side, i, b):
        return (((kind * 2 + side) * 10 + i) * BRICKS + b) * PITCH

    across = BRICKS * PITCH
    for side in range(2):
        for deep in (7, 16):
            field[pl.ds(cell(2, side, 1, 0) + deep, 16, stride=PITCH)] = jnp.zeros((16, CH), jnp.float32)
        for kind in (1, 2):
            for i in (0, 9):
                halos[kind, side, i] = jnp.zeros((BRICKS * EDGE, 3 * CH), jnp.bfloat16)
    for b in range(BRICKS):
        for k, (dx, dy, dz) in enumerate(DIRECTIONS):
            base = pl.multiple_of(faces[b, k], FACE)
            cut = lambda d: 7 if d < 0 else 0
            put = lambda d: 0 if d < 0 else 9
            deep = 7 if dz < 0 else 16
            kind = 0 if dx != 0 else 1 if dy != 0 else 2
            side = 0 if (dx, dy, dz)[kind] < 0 else 1
            if kind == 0 and dy != 0:
                there = cell(0, side, put(dy), b)
                if dz == 0:
                    field[pl.ds(there + 8, 8)] = table[pl.ds(base + cut(dy) * 8, 8)]
                else:
                    field[pl.ds(there + deep, 1)] = table[pl.ds(base + cut(dy) * 8 + cut(dz), 1)]
            elif kind < 2 and dz != 0:
                column = table[pl.ds(base + cut(dz), 8, stride=8)]
                field[pl.ds(cell(kind, side, 1, b) + deep, 8, stride=across)] = column
            else:
                for i in range(EDGE):
                    field[pl.ds(cell(kind, side, i + 1, b) + 8, 8)] = table[pl.ds(base + i * 8, 8)]
    for kind in range(3):
        for side in range(2):
            for i in range(10) if kind == 0 else range(1, 9):
                for w in range(3):
                    tile = jnp.concatenate(
                        [field[pl.ds(cell(kind, side, i, b) + 7 + w, 8)] for b in range(BRICKS)], axis=0
                    )
                    halos[kind, side, i, :, w * CH : (w + 1) * CH] = tile.astype(jnp.bfloat16)


def add_halos(halos, weights, acc):
    rows = EDGE * BRICKS * EDGE
    for kind in range(3):
        wide = jnp.concatenate([halos[kind, :, s : s + 8] for s in range(3)], axis=-1)
        sides = []
        for near in (0, 2):
            taps = []
            for s in range(3):
                for w in range(3):
                    tap = [(near * 3 + s) * 3 + w, (s * 3 + near) * 3 + w, (s * 3 + w) * 3 + near][kind]
                    taps.append(weights[pl.ds(tap * CH, CH)])
            sides.append(jnp.concatenate(taps, axis=0))
        part = jnp.dot(
            wide.reshape(2 * rows, 9 * CH), jnp.concatenate(sides, axis=1), preferred_element_type=jnp.float32
        )
        for side, edge in ((0, 0), (1, 7)):
            own = part[side * rows : (side + 1) * rows, side * CH : (side + 1) * CH]
            if kind == 0:
                acc[pl.ds(edge * rows, rows)] += own
                continue
            for x in range(EDGE):
                if kind == 1:
                    acc[pl.ds(x * rows + edge * 16, 16)] += own[x * 16 : x * 16 + 16]
                    continue
                for b in range(BRICKS):
                    line = pl.ds(x * rows + b * 8 + edge, 8, stride=16)
                    acc[line] = acc[line] + own[(x * 2 + b) * 8 : (x * 2 + b) * 8 + 8]


def convolve(window, weights, wide, total):
    rows = jnp.concatenate([window[p : p + 8] for p in range(3)], axis=-1).reshape(BRICKS * VOX, 9 * CH)
    taps = [
        jnp.concatenate([weights[pl.ds((p * 3 + t) * 3 * CH, 3 * CH)] for p in range(3)], axis=0) for t in range(3)
    ]
    wide[...] = jnp.dot(rows, jnp.concatenate(taps, axis=1), preferred_element_type=jnp.float32)
    line = BRICKS * EDGE
    for x in range(EDGE):
        for y in range(EDGE):
            here = (x * EDGE + y) * line
            value = wide[pl.ds(here, line), CH : 2 * CH]
            if y > 0:
                value = value + wide[pl.ds(here - line, line), :CH]
            if y < 7:
                value = value + wide[pl.ds(here + line, line), 2 * CH :]
            total[x * EDGE + y] = value.reshape(BRICKS, EDGE, CH)


def inner_kernel(step, act, weights_src, *rest):
    if step == 0:
        *tables_hbm, total, weights, faces, slots, window, wide, neighbours, kept, owner, sems = rest
        tables = (neighbours, kept, owner)
        copies = fetch(sems, (weights_src.at[0], weights), *zip(tables_hbm, tables))
        for copy in copies[1:]:
            copy.wait()
        find_routes(*tables, faces, slots)
    else:
        total, window, wide = rest
        weights = weights_src.at[step]
    blank = jnp.zeros((BRICKS * EDGE, 3 * CH), jnp.bfloat16)
    row = lax.broadcasted_iota(jnp.int32, (EDGE, CH), 0)
    for x in range(10):
        for y in range(8):
            if not 0 < x < 9:
                window[x, y] = blank
                continue
            here = pl.ds(((x - 1) * 8 + y) * 8, 8)
            tiles = [act[b, here].astype(jnp.float32) for b in range(BRICKS)]
            shifts = (
                [jnp.where(row > 0, pltpu.roll(t, 1, 0), 0.0) for t in tiles],
                tiles,
                [jnp.where(row < 7, pltpu.roll(t, 7, 0), 0.0) for t in tiles],
            )
            for w in range(3):
                window[x, y, :, w * CH : (w + 1) * CH] = jnp.concatenate(shifts[w], axis=0).astype(jnp.bfloat16)
    if step == 0:
        copies[0].wait()
    convolve(window, weights, wide, total)


def conv_kernel(
    step, faces, last, first, core, rng, slab_a, slab_b, total, weights, gain_hbm, shift_hbm, *rest,
):
    rest = list(rest)
    state = rest.pop(0) if step % 2 else None
    slots = rest.pop(0) if step == 3 else None
    if step == 3:
        packed = rest.pop(0)
    else:
        act_out = rest.pop(0)
        sends = [rest.pop(0) for _ in range(6)]
        state_out = rest.pop(0) if step == 1 else None
    table, field, halos, acc, result, act_s, gain, shift, sems = rest
    copies = fetch(sems, (gain_hbm, gain), (shift_hbm, shift)) if step < 3 else []
    gather_halos(faces, (last, first, core, rng, slab_a, slab_b), table, field, halos)
    acc[...] = total[...].reshape(BRICKS * VOX, CH)
    add_halos(halos, weights.at[step] if step else weights, acc)
    if step == 3:
        packed[...] = jnp.zeros(packed.shape, packed.dtype)
    for copy in copies:
        copy.wait()
    for b in range(BRICKS):
        value = acc[...].reshape(OCT, BRICKS, EDGE, CH)[:, b]
        if step % 2:
            value = value + state[b].astype(jnp.float32).reshape(OCT, EDGE, CH)
        value = value.astype(jnp.bfloat16)
        if step == 1:
            state_out[b] = value.reshape(VOX, CH)
        result[b] = value.astype(jnp.float32)
        if step < 3:
            load = lambda b=b: result[b]
            emit_active(load, b, gain[step + 1 : step + 2], shift[step + 1 : step + 2], act_s, act_out, sends)
    if step < 3:
        choose_sends(sends)
        return
    low = lax.broadcasted_iota(jnp.int32, (4, 2, 8, CH), 2) < 4
    for b in range(BRICKS):
        for ox in range(2):
            for oy in range(2):
                tiles = result[b, pl.ds(ox * 32, 32)].reshape(4, 8, EDGE, CH)
                tiles = tiles[:, oy * 4 : oy * 4 + 4].reshape(4, 2, 2, EDGE, CH)
                even, odd = tiles[:, :, 0], tiles[:, :, 1]
                turn = lambda v: pltpu.roll(v.reshape(8, EDGE, CH), 4, 1).reshape(4, 2, EDGE, CH)
                for oz in range(2):
                    block = jnp.where(low, even, turn(odd)) if oz == 0 else jnp.where(low, turn(even), odd)
                    child = b * 8 + (ox * 2 + oy) * 2 + oz
                    block = block.reshape(OCT, CH).astype(jnp.bfloat16)
                    slot = slots[child]

                    @pl.when(slot >= 0)
                    def _(slot=slot, block=block):
                        packed[slot] = block


def grow_kernel(octants, up, out, grown, sems):
    copies = []
    for i in range(PARTS):
        part = pl.ds(i * (128 // PARTS), 128 // PARTS)
        rows = octants[part].reshape(-1, CH)
        value = jnp.dot(rows, up[...], preferred_element_type=jnp.float32)
        grown[part] = value.astype(jnp.bfloat16).reshape(128 // PARTS, OCT, 4 * CH)
        copies.append(pltpu.make_async_copy(grown.at[part], out.at[part], sems.at[i]))
        copies[-1].start()
    for copy in copies:
        copy.wait()


def bf16(*shape):
    return jax.ShapeDtypeStruct(shape, jnp.bfloat16)


def swap(block, axis, odd):
    slabs, ranges = lax.axis_size("slab"), lax.axis_size("range")
    route = []
    for s in range(slabs):
        for r in range(ranges):
            step = 1 if (s if axis == "slab" else r) % 2 == odd else -1
            to = [s + step, r] if axis == "slab" else [s, r + step]
            if not 0 <= to[0] < slabs:
                to = [s, r ^ 1]
            if not 0 <= to[1] < ranges:
                to = [s ^ 1, r]
            route.append((s * ranges + r, to[0] * ranges + to[1]))
    return lax.ppermute(block, ("slab", "range"), route)


def exchange(sends):
    last, first, to_core, to_range, to_a, to_b = sends
    rng = swap(to_range, "range", True)
    slab_b = swap(to_b, "slab", True)
    slab_a = swap(to_a, "slab", False)
    core = swap(to_core, "range", False)
    return last, first, core, rng, slab_a, slab_b


SENDS = [
    bf16(3, BRICKS, FACE, CH),
    bf16(3, BRICKS, FACE, CH),
    bf16(3, BRICKS, FACE, CH),
    bf16(3, BRICKS, FACE, CH),
    bf16(BRICKS, FACE, CH),
    bf16(BRICKS, FACE, CH),
]
LIMIT = 16 * 1024 * 1024
PARTS = 16


def shards(features, neighbours, keep_mask, owner, norm_gain, norm_shift, conv_weights, up_weight):
    act_s = pltpu.VMEM((BRICKS * VOX, CH), jnp.float32)
    norm_s = [pltpu.VMEM((4, CH), jnp.float32)] * 2
    in_hbm = lambda v: pltpu.with_memory_space_constraint(v, pltpu.HBM)
    gain, shift = in_hbm(norm_gain), in_hbm(norm_shift)
    act, *sends = pl.pallas_call(
        start_kernel,
        out_shape=[bf16(BRICKS, VOX, CH), *SENDS],
        in_specs=[HBM] * 3,
        out_specs=[VMEM] * 7,
        scratch_shapes=[
            act_s,
            pltpu.VMEM((BRICKS, VOX, CH), jnp.bfloat16),
            *norm_s,
            pltpu.SemaphoreType.DMA((2 + BRICKS,)),
        ],
        compiler_params=pltpu.CompilerParams(vmem_limit_bytes=LIMIT),
        cost_estimate=pl.CostEstimate(flops=10**7, bytes_accessed=2**22, transcendentals=2**17),
        name="start",
    )(in_hbm(features), gain, shift)
    all_weights = conv_weights.reshape(4, 27 * CH, CH)
    state = features
    for step in range(4):
        planes = exchange(sends)
        window_s = [
            pltpu.VMEM((10, 8, BRICKS * EDGE, 3 * CH), jnp.bfloat16),
            pltpu.VMEM((BRICKS * VOX, 3 * CH), jnp.float32),
        ]
        call = functools.partial(
            pl.pallas_call,
            functools.partial(inner_kernel, step),
            compiler_params=pltpu.CompilerParams(vmem_limit_bytes=LIMIT),
            cost_estimate=pl.CostEstimate(flops=2 * 10**9, bytes_accessed=2**21, transcendentals=0),
        )
        total_t = jax.ShapeDtypeStruct((OCT, BRICKS, EDGE, CH), jnp.float32)
        if step == 0:
            total, weights, faces, slots = call(
                out_shape=[
                    total_t,
                    bf16(27 * CH, CH),
                    jax.ShapeDtypeStruct((BRICKS, 26), jnp.int32),
                    jax.ShapeDtypeStruct((8 * BRICKS,), jnp.int32),
                ],
                in_specs=[VMEM] + [HBM] * 4,
                out_specs=[VMEM, VMEM, SMEM, SMEM],
                scratch_shapes=[
                    *window_s,
                    pltpu.SMEM((BRICKS, 26), jnp.int32),
                    pltpu.SMEM((BRICKS, 8), jnp.int32),
                    pltpu.SMEM((BRICKS, 8), jnp.int32),
                    pltpu.SemaphoreType.DMA((4,)),
                ],
            )(act, in_hbm(all_weights), in_hbm(neighbours), in_hbm(keep_mask), in_hbm(owner))
        else:
            weights = all_weights
            (total,) = call(
                out_shape=[total_t], in_specs=[VMEM, VMEM], out_specs=[VMEM], scratch_shapes=window_s
            )(act, weights)
        inputs = [faces, *planes, total, weights, gain, shift]
        in_specs = [SMEM] + [VMEM] * 8 + [HBM] * 2
        if step % 2:
            inputs.append(state)
            in_specs.append(VMEM)
        if step == 3:
            inputs.append(slots)
            in_specs.append(SMEM)
            outs = [bf16(128, OCT, CH)]
        else:
            outs = [bf16(BRICKS, VOX, CH), *SENDS]
            if step == 1:
                outs.append(bf16(BRICKS, VOX, CH))
        result = pl.pallas_call(
            functools.partial(conv_kernel, step),
            out_shape=outs,
            in_specs=in_specs,
            out_specs=[VMEM] * len(outs),
            scratch_shapes=[
                pltpu.VMEM((FACES * FACE, CH), jnp.float32),
                pltpu.VMEM((6 * 10 * BRICKS * PITCH, CH), jnp.float32),
                pltpu.VMEM((3, 2, 10, BRICKS * EDGE, 3 * CH), jnp.bfloat16),
                pltpu.VMEM((BRICKS * VOX, CH), jnp.float32),
                pltpu.VMEM((BRICKS, OCT, EDGE, CH), jnp.float32),
                act_s,
                *norm_s,
                pltpu.SemaphoreType.DMA((2,)),
            ],
            compiler_params=pltpu.CompilerParams(vmem_limit_bytes=LIMIT),
            cost_estimate=pl.CostEstimate(flops=5 * 10**8, bytes_accessed=2**22, transcendentals=2**17),
        )(*inputs)
        if step < 3:
            act, sends = result[0], result[1:7]
            if step == 1:
                state = result[7]
    arrived = lax.all_to_all(result[0], "range", split_axis=0, concat_axis=0, tiled=True)
    return pl.pallas_call(
        grow_kernel,
        out_shape=bf16(128, OCT, 4 * CH),
        in_specs=[VMEM, VMEM],
        out_specs=HBM,
        scratch_shapes=[pltpu.VMEM((128, OCT, 4 * CH), jnp.bfloat16), pltpu.SemaphoreType.DMA((PARTS,))],
        compiler_params=pltpu.CompilerParams(vmem_limit_bytes=32 * 1024 * 1024),
        name="grow",
    )(arrived, up_weight)


def solution(mesh):
    split = P(("slab", "range"))
    return jax.shard_map(
        shards,
        mesh=mesh,
        in_specs=(split, split, split, split, P(), P(), P(), P()),
        out_specs=split,
        check_vma=False,
    )
```
